128 devices in a mesh: orb: 16 (over z, x), comp: 8 (over y, core).
Axes of the slice: x: 4, y: 4, z: 4, core: 2. Of those that a mesh axis runs over, the one named last changes fastest.
Arguments:
- psi: bfloat16 [1024, 4, 128, 256], P('orb', None, 'comp'), may hold values from -16 to 16
- region_start: int32 [1024], replicated, may hold values from 0 to 63
- region_len: int32 [1024], replicated, may hold values from 32 to 64
- fine_mask: int32 [128, 16], P('comp'), may hold values 0 or 1
- occupation: int32 [1024], replicated, may hold values from 0 to 2
- kinetic_taps: bfloat16 [29, 4, 4], replicated, may hold values from -0.5 to 0.5
- magic_taps: bfloat16 [16, 4], replicated, may hold values from -0.75 to 0.75
- external: float32 [128, 256], P('comp'), may hold values from -12 to 12
Outputs:
- density: float32 [128, 256], P('comp', 'orb')
- psi_next: bfloat16 [1024, 4, 128, 256], P(None, None, 'comp', 'orb')
The draws below stay inside these ranges and needn't reach their ends.
Inputs may be any that keep to these rules, and one draw needn't show every extreme that they name: region_start + region_len <= 128.
All inputs are finite; a program needn't handle non-finite values. No bound on the sum of `fine_mask` on one device may be relied on, other than what follows from the above.
Results may differ from the reference program's by a relative error of at most 0.012.
Values may be sent and summed in bfloat16 or wider, within the bound.
A program may use at most 128 MiB of HBM per device.

```python
import math
import jax
import jax.numpy as jnp
from jax import lax

CH = 4
TAPS = 29
MTAPS = 16
ZB = 16
ORB_DEV = 64
XD = 16
ZP = 16
NORB = 1024
GX = 128
GZ = 256
NZB = 16
GRID = 32768
N_ORB = 16


def draw_psi(key, part):
    key_scale = jax.random.fold_in(key, 71)
    key_noise = jax.random.fold_in(key, 72)
    levels = jax.random.uniform(key_scale, (NORB, 1, GX // XD, 1, GZ // ZP, 1), jnp.float32) * math.log(16.0)
    amplitude = jnp.exp(levels)
    amplitude = amplitude / jnp.sqrt(jnp.mean(amplitude * amplitude, axis=(2, 4), keepdims=True))
    shape = (NORB, CH, GX // XD, XD, GZ // ZP, ZP)
    noise = jnp.clip(jax.random.normal(key_noise, shape, jnp.float32), -6.0, 6.0)
    values = (amplitude * noise).reshape(NORB, CH, GX, GZ)
    return values.astype(jnp.bfloat16)


def set_ends(array, rng, least, largest):
    dims = array.shape
    spot = [jax.random.randint(jax.random.fold_in(rng, axis), (), 0, dims[axis]) for axis in range(len(dims))]
    array = array.at[tuple(spot)].set(least)
    longest = dims.index(max(dims))
    spot[longest] = (spot[longest] + 1) % dims[longest]
    return array.at[tuple(spot)].set(largest)


def block_levels(key, shape, cuts, smallest, largest):
    def one(axis_at, blocks):
        heights = jax.random.uniform(jax.random.fold_in(jax.random.fold_in(key, 6), axis_at), (blocks,), jnp.float32, smallest / len(cuts), largest / len(cuts))
        return jnp.repeat(jnp.exp(heights), shape[axis_at] // blocks).reshape((-1,) + (1,) * (len(shape) - axis_at - 1))

    gain = one(*cuts[0])
    for cut in cuts[1:]:
        gain = gain * one(*cut)
    return gain


def centred(own_key, dims, deviation, most, cuts=(), kind=jnp.bfloat16):
    array = deviation * jax.random.normal(own_key, dims, jnp.float32)
    if cuts:
        array = array * block_levels(own_key, dims, cuts, -0.22, 0.18)
    return jnp.clip(array, -most, most).astype(kind)


def setup_inputs(seed: int = 0) -> dict:
    keys = jax.random.split(jax.random.key(seed), 9)
    psi = draw_psi(jax.random.fold_in(keys[8], 71), 0)
    region_start = set_ends(jax.random.randint(keys[1], (NORB,), 0, GX // 2), jax.random.fold_in(keys[1], 1), 0, (GX // 2) - 1).astype(jnp.int32)
    region_len = set_ends(jax.random.randint(keys[2], (NORB,), GX // 4, GX // 2 + 1), jax.random.fold_in(keys[2], 1), GX // 4, (GX // 2 + 1) - 1).astype(jnp.int32)
    fine_mask = set_ends((jax.random.randint(keys[3], (GX, NZB), 0, 2) < 1).astype(jnp.int32), jax.random.fold_in(keys[3], 1), 0, 1)
    occupation = set_ends(jax.random.randint(keys[4], (NORB,), 0, 3), jax.random.fold_in(keys[4], 1), 0, 2).astype(jnp.int32)
    kinetic_taps = centred(keys[5], (TAPS, CH, CH), (TAPS * CH) ** -0.5, 0.5)
    magic_taps = centred(keys[6], (MTAPS, CH), (MTAPS * CH) ** -0.5, 0.75)
    external = centred(keys[7], (GX, GZ), 2.0, 12.0, ((0, 8),), jnp.float32)
    return {"psi": psi, "region_start": region_start, "region_len": region_len, "fine_mask": fine_mask, "occupation": occupation, "kinetic_taps": kinetic_taps, "magic_taps": magic_taps, "external": external}


xc_factor = 0.98474502
step_length = 0.1
highest = lax.Precision.HIGHEST


def conv_planes(values, filter_taps):
    half = (filter_taps.shape[0] - 1) // 2
    padded = jnp.pad(values, ((0, 0), (0, 0), (half, half), (0, 0)))
    total = jnp.zeros(values.shape, jnp.float32)
    for position in range(filter_taps.shape[0]):
        total = total + jnp.einsum("ed,bdxz->bexz", filter_taps[position], padded[:, :, position:position + GX, :], precision=highest)
    return total


def conv_depth(values, filter_taps):
    half = (filter_taps.shape[0] - 1) // 2
    padded = jnp.pad(values, ((0, 0), (0, 0), (0, 0), (half, half)))
    total = jnp.zeros(values.shape, jnp.float32)
    for position in range(filter_taps.shape[0]):
        total = total + jnp.einsum("ed,bdxz->bexz", filter_taps[position], padded[:, :, :, position:position + GZ], precision=highest)
    return total


def magic_forward(values, magic):
    padded = jnp.pad(values, ((0, 0), (0, 0), (0, 0), (14, 14)))
    total = jnp.zeros((values.shape[0], GX, GZ), jnp.float32)
    for position in range(MTAPS):
        total = total + jnp.einsum("d,bdxz->bxz", magic[position], padded[:, :, :, position + 7:position + 7 + GZ], precision=highest)
    return total


def magic_adjoint(weighted, magic):
    padded = jnp.pad(weighted, ((0, 0), (0, 0), (14, 14)))
    total = jnp.zeros((weighted.shape[0], CH, GX, GZ), jnp.float32)
    for position in range(MTAPS):
        total = total + magic[position][None, :, None, None] * padded[:, None, :, 21 - position:21 - position + GZ]
    return total


def reference(psi, region_start, region_len, fine_mask, occupation, kinetic_taps, magic_taps, external):
    planes = jnp.arange(GX).astype(jnp.int32)
    inside = (planes[None, :] >= region_start[:, None]) & (planes[None, :] < (region_start + region_len)[:, None])
    fine_cells = jnp.repeat(fine_mask, ZB, axis=1)
    channel_on = (jnp.arange(CH)[:, None, None] == 0) | (fine_cells[None] > 0)
    kinetic_f = kinetic_taps.astype(jnp.float32)
    magic_f = magic_taps.astype(jnp.float32)
    blocks_psi = psi.reshape(N_ORB, ORB_DEV, CH, GX, GZ)
    blocks_in = inside.reshape(N_ORB, ORB_DEV, GX)

    def first(pair):
        block_psi, block_in = pair
        support = block_in[:, None, :, None] & channel_on[None]
        masked = jnp.where(support, block_psi, jnp.zeros((), block_psi.dtype))
        return masked, magic_forward(masked.astype(jnp.float32), magic_f)

    masked, grid_values = lax.map(first, (blocks_psi, blocks_in))
    occupied = occupation.astype(jnp.float32).reshape(N_ORB, ORB_DEV)
    density = jnp.sum(occupied[:, :, None, None] * grid_values * grid_values, axis=(0, 1))
    potential = external - xc_factor * jnp.cbrt(density)

    def second(triple):
        block_masked, block_values, block_in = triple
        support = block_in[:, None, :, None] & channel_on[None]
        weighted = (potential[None] * block_values).astype(jnp.bfloat16)
        weighted = lax.optimization_barrier(weighted)
        values = block_masked.astype(jnp.float32)
        total = conv_planes(values, kinetic_f) + conv_depth(values, kinetic_f)
        total = total + magic_adjoint(weighted.astype(jnp.float32), magic_f)
        return jnp.where(support, total, jnp.zeros((), jnp.float32)).astype(jnp.bfloat16)

    applied = lax.map(second, (masked, grid_values, blocks_in))
    masked_rows = masked.reshape(NORB, -1)
    applied_rows = applied.reshape(NORB, -1)
    intersection = jnp.dot(masked_rows, masked_rows.T, preferred_element_type=jnp.float32) / GRID
    lagrange = jnp.dot(applied_rows, masked_rows.T, preferred_element_type=jnp.float32) / GRID
    gradient = applied_rows.astype(jnp.float32) - jnp.dot(lagrange.astype(jnp.bfloat16), masked_rows, preferred_element_type=jnp.float32)
    trial = (masked_rows.astype(jnp.float32) - step_length * gradient).astype(jnp.bfloat16)
    trial = lax.optimization_barrier(trial)
    following = 1.5 * trial.astype(jnp.float32) - 0.5 * jnp.dot(intersection.astype(jnp.bfloat16), trial, preferred_element_type=jnp.float32)
    return density, following.astype(jnp.bfloat16).reshape(NORB, CH, GX, GZ)
```

```python
import functools

import jax
import jax.numpy as jnp
from jax import lax
from jax.experimental import pallas as pl
from jax.experimental.pallas import tpu as pltpu
from jax.sharding import PartitionSpec as P

ZB = 16


xc_factor = 0.98474502
step_length = 0.1


def padded(x, sides, width):
    edges = {}
    for axis, dim in sides:
        count, length = (lax.axis_size(axis), x.shape[dim])
        up = [(i, (i + 1) % count) for i in range(count - 1)]
        last = lax.slice_in_dim(x, length - width, length, axis=dim)
        first = lax.slice_in_dim(x, 0, width, axis=dim)
        edges[dim] = (
            lax.ppermute(last, axis, up),
            lax.ppermute(first, axis, [(b, a) for a, b in up]),
        )
    done = []
    for _, dim in sides:
        low, high = edges[dim]
        around = [(width, width) if d in done else (0, 0) for d in range(x.ndim)]
        x = jnp.concatenate([jnp.pad(low, around), x, jnp.pad(high, around)], axis=dim)
        done.append(dim)
    return x


def extended(cells, sides, width):
    for axis, dim in sides:
        count = lax.axis_size(axis)
        ends = count - 1
        head = lax.slice_in_dim(cells, 0, width, axis=dim)
        tail = lax.slice_in_dim(cells, cells.shape[dim] - width, cells.shape[dim], axis=dim)
        cells = jnp.concatenate(
            [
                lax.ppermute(tail, axis, [(i, (i + 1) % count) for i in range(ends)]),
                cells,
                lax.ppermute(head, axis, [((i + 1) % count, i) for i in range(ends)]),
            ],
            axis=dim,
        )
    return cells


MESH = pl.DeviceIdType.MESH


def coords():
    orb, comp = lax.axis_index("orb"), lax.axis_index("comp")
    return orb // 4, orb % 4, comp // 2, comp % 2


def at(z, x, y, core):
    return {"orb": z * 4 + x, "comp": y * 2 + core}


def turned(pos, axis, step):
    pos = list(pos)
    pos[axis] = lax.rem(pos[axis] + step, 4)
    return tuple(pos)


GROUPS = ((0, 768, 2, (0, 1)), (768, 768, 1, (2, 0)), (1536, 512, 0, (2, 1)))


def greet(targets):
    barrier = pltpu.get_barrier_semaphore()
    for t in targets:
        pl.semaphore_signal(barrier, inc=1, device_id=t, device_id_type=MESH)
    pl.semaphore_wait(barrier, len(targets))


def reduce_kernel(scale, w_ref, out_ref, h_in, h_sum, *rest):
    q_in, q_sum, f_in, f_sum = rest[0:3], rest[3:6], rest[6:9], rest[9:12]
    s0, r0, s1, r1, s2, r2, t2, u2, t1, u1, t0, u0 = rest[12:]
    here = coords()
    core = here[3]
    mate = at(here[0], here[1], here[2], 1 - core)
    targets = [mate]
    for a in (0, 1, 2):
        targets += [at(*turned(here, a, s)) for s in (1, 2, 3)]
    for a, b in ((0, 1), (0, 2), (1, 2)):
        targets += [at(*turned(turned(here, a, s), b, t)) for s in (1, 2, 3) for t in (1, 2, 3)]
    greet(targets)
    keep = pl.multiple_of(core * 512, 512)
    give = pl.multiple_of(512 - core * 512, 512)

    def remote(src, dst, ssem, rsem, to):
        return pltpu.make_async_remote_copy(
            src_ref=src, dst_ref=dst, send_sem=ssem, recv_sem=rsem, device_id=to, device_id_type=MESH
        )

    first = []
    for g, (col, width, axis, plane) in enumerate(GROUPS):
        c = remote(w_ref.at[pl.ds(give, 512), pl.ds(col, width)], h_in.at[:, pl.ds(col, width)], s0.at[g], r0.at[g], mate)
        c.start()
        first.append(c)
    second = []
    for g, (col, width, axis, plane) in enumerate(GROUPS):
        first[g].wait()

        def add(i, _, col=col, width=width):
            rows = pl.ds(pl.multiple_of(i * 32, 32), 32)
            mine = pl.ds(pl.multiple_of(keep + i * 32, 32), 32)
            total = w_ref[mine, pl.ds(col, width)].astype(jnp.float32) + h_in[rows, pl.ds(col, width)].astype(jnp.float32)
            h_sum[rows, pl.ds(col, width)] = total.astype(jnp.bfloat16)
            return 0

        lax.fori_loop(0, 16, add, 0)
        copies = []
        for s in (1, 2, 3):
            to = turned(here, axis, s)
            rows = pl.ds(pl.multiple_of(to[axis] * 128, 128), 128)
            c = remote(h_sum.at[rows, pl.ds(col, width)], q_in[g].at[s - 1], s1.at[g, s - 1], r1.at[g, s - 1], at(*to))
            c.start()
            copies.append(c)
        second.append(copies)
    third = []
    for g, (col, width, axis, plane) in enumerate(GROUPS):
        for c in second[g]:
            c.wait_recv()
        base = pl.multiple_of(here[axis] * 128, 128)

        def add(i, _, g=g, col=col, width=width, base=base):
            rows = pl.ds(pl.multiple_of(i * 16, 16), 16)
            total = h_sum[pl.ds(pl.multiple_of(base + i * 16, 16), 16), pl.ds(col, width)].astype(jnp.float32)
            for s in range(3):
                total = total + q_in[g][s, rows, :].astype(jnp.float32)
            q_sum[g][rows, :] = total.astype(jnp.bfloat16)
            return 0

        lax.fori_loop(0, 8, add, 0)
        half = width // 2
        copies = []
        n = 0
        for s in range(4):
            for t in range(4):
                if s == 0 and t == 0:
                    continue
                to = turned(turned(here, plane[0], s), plane[1], t)
                b = to[plane[0]] * 4 + to[plane[1]]
                piece = (pl.ds(pl.multiple_of((b // 2) * 16, 16), 16), pl.ds(pl.multiple_of((b % 2) * half, 128), half))
                c = remote(q_sum[g].at[piece[0], piece[1]], f_in[g].at[n], s2.at[g, n], r2.at[g, n], at(*to))
                c.start()
                copies.append(c)
                n += 1
        third.append(copies)
    fourth = []
    for g, (col, width, axis, plane) in enumerate(GROUPS):
        half = width // 2
        for c in third[g]:
            c.wait_recv()
        b = here[plane[0]] * 4 + here[plane[1]]
        total = q_sum[g][
            pl.ds(pl.multiple_of((b // 2) * 16, 16), 16), pl.ds(pl.multiple_of((b % 2) * half, 128), half)
        ].astype(jnp.float32)
        for n in range(15):
            total = total + f_in[g][n].astype(jnp.float32)
        f_sum[g][...] = (total * scale).astype(jnp.bfloat16)
        spot = out_ref.at[
            pl.ds(pl.multiple_of(keep + here[axis] * 128 + (b // 2) * 16, 16), 16),
            pl.ds(pl.multiple_of(col + (b % 2) * half, 128), half),
        ]
        copies = []
        n = 0
        for s in range(4):
            for t in range(4):
                if s == 0 and t == 0:
                    continue
                to = turned(turned(here, plane[0], s), plane[1], t)
                c = remote(f_sum[g], spot, t2.at[g, n], u2.at[g, n], at(*to))
                c.start()
                copies.append(c)
                n += 1
        own = pltpu.make_async_copy(f_sum[g], spot, t2.at[g, 15])
        own.start()
        fourth.append((own, copies))
    fifth = []
    for g, (col, width, axis, plane) in enumerate(GROUPS):
        own, copies = fourth[g]
        own.wait()
        for c in copies:
            c.wait_recv()
        spot = out_ref.at[pl.ds(pl.multiple_of(keep + here[axis] * 128, 128), 128), pl.ds(col, width)]
        copies = []
        for s in (1, 2, 3):
            c = remote(spot, spot, t1.at[g, s - 1], u1.at[g, s - 1], at(*turned(here, axis, s)))
            c.start()
            copies.append(c)
        fifth.append(copies)
    last = []
    for g, (col, width, axis, plane) in enumerate(GROUPS):
        for c in fifth[g]:
            c.wait_recv()
        spot = out_ref.at[pl.ds(keep, 512), pl.ds(col, width)]
        c = remote(spot, spot, t0.at[g], u0.at[g], mate)
        c.start()
        last.append(c)
    for g in range(3):
        last[g].wait()
        for c in second[g] + third[g] + fourth[g][1] + fifth[g]:
            c.wait_send()


def reduced(w, scale):
    bf = jnp.bfloat16
    dma = pltpu.SemaphoreType.DMA
    widths = [g[1] for g in GROUPS]
    return pl.pallas_call(
        functools.partial(reduce_kernel, scale),
        out_shape=jax.ShapeDtypeStruct(w.shape, bf),
        in_specs=[pl.BlockSpec(memory_space=pltpu.VMEM)],
        out_specs=pl.BlockSpec(memory_space=pltpu.VMEM),
        scratch_shapes=[pltpu.VMEM((512, 2048), bf), pltpu.VMEM((512, 2048), bf)]
        + [pltpu.VMEM((3, 128, w), bf) for w in widths]
        + [pltpu.VMEM((128, w), bf) for w in widths]
        + [pltpu.VMEM((15, 16, w // 2), bf) for w in widths]
        + [pltpu.VMEM((16, w // 2), bf) for w in widths]
        + [dma((3,)), dma((3,)), dma((3, 3)), dma((3, 3)), dma((3, 15)), dma((3, 15))]
        + [dma((3, 16)), dma((3, 15)), dma((3, 3)), dma((3, 3)), dma((3,)), dma((3,))],
        compiler_params=pltpu.CompilerParams(collective_id=7, has_side_effects=True, vmem_limit_bytes=40 << 20),
        name="reduce_pairs",
    )(w)


def onehot_band(window, length, shift, sign, count):
    offset = sign * (jnp.arange(window)[:, None] - jnp.arange(length)[None, :]) + shift
    return (offset[:, :, None] == jnp.arange(count)[None, None, :]).astype(jnp.bfloat16)


def kinetic_kernel(filter_taps, window, length):
    onehot = onehot_band(window, length, 0, 1, filter_taps.shape[0])
    return jnp.einsum(
        "jit,ted->djei", onehot, filter_taps, preferred_element_type=jnp.float32
    ).astype(jnp.bfloat16)


def magic_kernel(magic, window, length):
    onehot = onehot_band(window, length, -7, 1, magic.shape[0])
    return jnp.einsum("jit,td->dji", onehot, magic, preferred_element_type=jnp.float32).astype(
        jnp.bfloat16
    )


def adjoint_kernel(magic, window, length):
    onehot = onehot_band(window, length, 21, -1, magic.shape[0])
    return jnp.einsum("jit,te->jei", onehot, magic, preferred_element_type=jnp.float32).astype(
        jnp.bfloat16
    )


def region_support(starts, lengths, first_plane, slab_len, fine_cells, channels):
    planes = first_plane + jnp.arange(slab_len)
    inside = (planes[None, :] >= starts[:, None]) & (planes[None, :] < (starts + lengths)[:, None])
    channel_on = (jnp.arange(channels)[:, None, None] == 0) | (fine_cells[None] > 0)
    return inside[:, None, :, None] & channel_on[None]


def plane_conv(plane_window, filter_taps, slab_len):
    kernel = kinetic_kernel(filter_taps, plane_window.shape[2], slab_len)
    return jnp.einsum("odjz,djei->oeiz", plane_window, kernel, preferred_element_type=jnp.float32)


def depth_apply(depth_window, filter_taps, magic, cells_out):
    window = depth_window.shape[-1]
    block_len = window - 28
    kernel = kinetic_kernel(filter_taps, window, block_len)
    forward = magic_kernel(magic, window, block_len)
    kinetic = jnp.einsum(
        "odxbj,djei->oexbi", depth_window, kernel, preferred_element_type=jnp.float32
    )
    grid_values = jnp.einsum(
        "odxbj,dji->oxbi", depth_window, forward, preferred_element_type=jnp.float32
    )
    shape = depth_window.shape
    return (
        kinetic.reshape(shape[0], shape[1], shape[2], cells_out),
        grid_values.reshape(shape[0], shape[2], cells_out),
    )


def adjoint_apply(value_window, magic, channels, cells_out):
    window = value_window.shape[-1]
    kernel = adjoint_kernel(magic, window, window - 28)
    result = jnp.einsum("oxbj,jei->oexbi", value_window, kernel, preferred_element_type=jnp.float32)
    return result.reshape(value_window.shape[0], channels, value_window.shape[1], cells_out)


def local(psi, region_start, region_len, fine_mask, occupation, kinetic_taps, magic_taps, external):
    orb_dev, channels, slab_len, cells_z = psi.shape
    orb_count = lax.axis_size("orb")
    comp_count = lax.axis_size("comp")
    orbitals = orb_dev * orb_count
    piece_len = cells_z // orb_count
    grid_cells = slab_len * comp_count * cells_z
    first_plane = lax.axis_index("comp") * slab_len
    first_cell = lax.axis_index("orb") * piece_len
    first_orbital = lax.axis_index("orb") * orb_dev
    fine_cells = jnp.repeat(fine_mask, ZB, axis=1)
    starts = lax.dynamic_slice_in_dim(region_start, first_orbital, orb_dev)
    lengths = lax.dynamic_slice_in_dim(region_len, first_orbital, orb_dev)
    support = region_support(starts, lengths, first_plane, slab_len, fine_cells, channels)
    masked = jnp.where(support, psi, jnp.zeros((), psi.dtype))
    masked_t = lax.all_to_all(masked, "orb", split_axis=3, concat_axis=0, tiled=True)
    fine_piece = lax.dynamic_slice_in_dim(fine_cells, first_cell, piece_len, 1)
    support_t = region_support(
        region_start, region_len, first_plane, slab_len, fine_piece, channels
    )
    grid_window = padded(masked_t, (("orb", 3), ("comp", 2)), 14)
    kinetic, grid_values = depth_apply(
        grid_window[:, :, 14 : 14 + slab_len, None, :], kinetic_taps, magic_taps, piece_len
    )
    kinetic = kinetic + plane_conv(
        grid_window[:, :, :, 14 : 14 + piece_len], kinetic_taps, slab_len
    )
    occupied = occupation.astype(jnp.float32)
    density = jnp.sum(occupied[:, None, None] * grid_values * grid_values, axis=0)
    outer = lax.dynamic_slice_in_dim(external, first_cell, piece_len, 1)
    potential = outer - xc_factor * jnp.cbrt(density)
    weighted = (potential[None] * grid_values).astype(jnp.bfloat16)
    value_window = extended(weighted, (("orb", 2),), 14)
    total_applied = kinetic + adjoint_apply(
        value_window[:, :, None, :], magic_taps, channels, piece_len
    )
    applied_t = jnp.where(support_t, total_applied, jnp.zeros((), jnp.float32)).astype(jnp.bfloat16)
    masked_k = jnp.transpose(masked_t, (1, 2, 3, 0)).reshape(-1, orbitals)
    applied_k = jnp.transpose(applied_t, (1, 2, 3, 0)).reshape(-1, orbitals)
    intersection_part = jnp.einsum("kj,ki->ji", masked_k, masked_k, preferred_element_type=jnp.float32)
    lagrange_part = jnp.einsum("kj,ki->ji", masked_k, applied_k, preferred_element_type=jnp.float32)
    both = reduced(
        jnp.concatenate([intersection_part.astype(jnp.bfloat16), lagrange_part.astype(jnp.bfloat16)], axis=1), 1.0 / grid_cells
    )
    intersection_round, lagrange_round = both[:, :orbitals], both[:, orbitals:]
    gradient = applied_k.astype(jnp.float32) - jnp.dot(masked_k, lagrange_round, preferred_element_type=jnp.float32)
    trial = (masked_k.astype(jnp.float32) - step_length * gradient).astype(jnp.bfloat16)
    following = 1.5 * trial.astype(jnp.float32) - 0.5 * jnp.dot(trial, intersection_round, preferred_element_type=jnp.float32)
    psi_next = jnp.transpose(
        following.astype(jnp.bfloat16).reshape(channels, slab_len, piece_len, orbitals), (3, 0, 1, 2)
    )
    return (density, psi_next)


def solution(mesh):
    return jax.shard_map(
        local,
        mesh=mesh,
        in_specs=(
            P("orb", None, "comp", None),
            P(),
            P(),
            P("comp", None),
            P(),
            P(),
            P(),
            P("comp", None),
        ),
        out_specs=(P("comp", "orb"), P(None, None, "comp", "orb")),
        check_vma=False,
    )
```

```python
import functools

import jax
import jax.numpy as jnp
from jax import lax
from jax.experimental import pallas as pl
from jax.experimental.pallas import tpu as pltpu
from jax.sharding import PartitionSpec as P

ZB = 16
xc_factor = 0.98474502
step_length = 0.1
f32, bf16 = jnp.float32, jnp.bfloat16

MESH = pl.DeviceIdType.MESH


def coords():
    orb, comp = lax.axis_index("orb"), lax.axis_index("comp")
    return orb // 4, orb % 4, comp // 2, comp % 2


def at(z, x, y, core):
    return {"orb": z * 4 + x, "comp": y * 2 + core}


def turned(pos, axis, step):
    pos = list(pos)
    pos[axis] = lax.rem(pos[axis] + step, 4)
    return tuple(pos)


def greet(targets):
    barrier = pltpu.get_barrier_semaphore()
    for t in targets:
        pl.semaphore_signal(barrier, inc=1, device_id=t, device_id_type=MESH)
    pl.semaphore_wait(barrier, len(targets))


def rows_at(i, size):
    return pl.ds(pl.multiple_of(i * size, size), size)


def eye(n):
    return (
        lax.broadcasted_iota(jnp.int32, (n, n), 0) == lax.broadcasted_iota(jnp.int32, (n, n), 1)
    ).astype(bf16)


def band(row):
    wide = jnp.broadcast_to(row, (256, 256))
    rolled = pltpu.roll(wide, 0, 1, stride=1, stride_axis=0)
    gap = lax.broadcasted_iota(jnp.int32, (256, 256), 0) - lax.broadcasted_iota(jnp.int32, (256, 256), 1)
    return jnp.where((gap <= 14) & (gap >= -14), rolled, 0.0).astype(bf16)


def inside_planes(start_ref, len_ref, first_orbital, first_plane, o):
    begin = start_ref[first_orbital + o] - first_plane
    plane = lax.broadcasted_iota(jnp.int32, (16, 256), 0)
    return (plane >= begin) & (plane < begin + len_ref[first_orbital + o])


def fine_points(fine_ref):
    spread = (
        lax.broadcasted_iota(jnp.int32, (16, 256), 1) // ZB == lax.broadcasted_iota(jnp.int32, (16, 256), 0)
    ).astype(bf16)
    return jnp.dot((fine_ref[...] > 0).astype(f32).astype(bf16), spread, preferred_element_type=f32)


def pack(wide_lo, wide_hi, pack_ref):
    unit = eye(256)

    def step(j, _):
        halves = []
        for ref in (wide_lo, wide_hi):
            halves.append(
                jnp.concatenate([ref[pl.ds(j, 64, stride=64), :], ref[pl.ds(j + 32, 64, stride=64), :]], axis=0)
            )
        both = jnp.concatenate(halves, axis=1).astype(bf16)
        turned_over = lax.dot_general(unit, both, (((1,), (1,)), ((), ())), preferred_element_type=f32).astype(bf16)
        for q in range(16):
            pack_ref[q, rows_at(j, 16), :] = turned_over[q * 16 : q * 16 + 16, :]
        return 0

    lax.fori_loop(0, 32, step, 0, unroll=4)


def first_kernel(start_ref, len_ref, occ_ref, psi_ref, fine_ref, base_ref, masked_ref, pack_ref, values_ref, part_ref, lo, hi):
    first_orbital = lax.axis_index("orb") * 64
    first_plane = lax.axis_index("comp") * 16
    fine = fine_points(fine_ref) > 0.5

    def mask(o, _):
        inside = inside_planes(start_ref, len_ref, first_orbital, first_plane, o)
        for c in range(4):
            on = inside if c == 0 else inside & fine
            value = jnp.where(on, psi_ref[o, c].astype(f32), 0.0)
            masked_ref[o, c] = value.astype(bf16)
            rows = pl.ds(pl.multiple_of(o * 64 + c * 16, 16), 16)
            lo[rows, :] = value[:, :128]
            hi[rows, :] = value[:, 128:]
        return 0

    lax.fori_loop(0, 64, mask, 0, unroll=2)
    forward = [band(base_ref[pl.ds(16 + d, 1), :]) for d in range(4)]

    def block(i, total):
        got = jnp.zeros((256, 256), f32)
        for d in range(4):
            rows = masked_ref[rows_at(i, 16), d].reshape(256, 256)
            got = got + jnp.dot(rows, forward[d], preferred_element_type=f32)
        for n in range(16):
            one = got[n * 16 : n * 16 + 16]
            values_ref[i * 16 + n] = one
            total = total + occ_ref[first_orbital + i * 16 + n].astype(f32) * (one * one)
        return total

    part_ref[...] = lax.fori_loop(0, 4, block, jnp.zeros((16, 256), f32))
    pack(lo, hi, pack_ref)


VM = pl.BlockSpec(memory_space=pltpu.VMEM)
SM = pl.BlockSpec(memory_space=pltpu.SMEM)
HB = pl.BlockSpec(memory_space=pl.ANY)


def shape(dims, kind=bf16):
    return jax.ShapeDtypeStruct(dims, kind)


def first_step(start, length, occupation, psi, fine, base):
    return pl.pallas_call(
        first_kernel,
        out_shape=(shape((64, 4, 16, 256)), shape((16, 512, 128)), shape((64, 16, 256), f32), shape((16, 256), f32)),
        in_specs=[SM, SM, SM, VM, VM, VM],
        out_specs=(VM, VM, VM, VM),
        scratch_shapes=[pltpu.VMEM((4096, 128), f32)] * 2,
        compiler_params=pltpu.CompilerParams(vmem_limit_bytes=40 << 20),
        name="first",
    )(start, length, occupation, psi, fine, base)


def plane_steps():
    return [(s, t) for s in range(4) for t in range(4) if s or t]


GROUPS = ((0, 1024, 2, (0, 1)), (1024, 512, 1, (0, 2)), (1536, 512, 0, (1, 2)))


def remote(src, dst, ssem, rsem, to):
    return pltpu.make_async_remote_copy(
        src_ref=src, dst_ref=dst, send_sem=ssem, recv_sem=rsem, device_id=to, device_id_type=MESH
    )


class Group:
    def __init__(self, g, scale, w_ref, out_ref, h_in, h_sum, q_in, q_sum, f_in, f_sum, sems):
        self.g, self.scale = g, scale
        self.w, self.out, self.h_in, self.h_sum = w_ref, out_ref, h_in, h_sum
        self.q_in, self.q_sum, self.f_in, self.f_sum = q_in, q_sum, f_in, f_sum
        self.sems = sems
        self.col, self.width, self.axis, self.plane = GROUPS[g]
        self.cols = pl.ds(self.col, self.width)
        self.here = coords()
        z, x, y, core = self.here
        self.mate = at(z, x, y, 1 - core)
        self.keep = pl.multiple_of(core * 512, 512)
        self.give = pl.multiple_of(512 - core * 512, 512)
        self.sent = []

    def begin(self):
        s0, r0 = self.sems[0:2]
        rows = pl.ds(self.give, 512)
        self.copy0 = remote(self.w.at[rows, self.cols], self.h_in.at[:, self.cols], s0.at[self.g], r0.at[self.g], self.mate)
        self.copy0.start()

    def to_axis(self):
        s1, r1 = self.sems[2:4]
        self.copy0.wait()

        def add(i, _):
            rows = rows_at(i, 32)
            mine = pl.ds(pl.multiple_of(self.keep + i * 32, 32), 32)
            total = self.w[mine, self.cols].astype(f32) + self.h_in[rows, self.cols].astype(f32)
            self.h_sum[rows, self.cols] = total.astype(bf16)
            return 0

        lax.fori_loop(0, 16, add, 0)
        self.copies1 = []
        for s in (2, 1, 3):
            to = turned(self.here, self.axis, s)
            rows = pl.ds(pl.multiple_of(to[self.axis] * 128, 128), 128)
            c = remote(self.h_sum.at[rows, self.cols], self.q_in.at[s - 1], s1.at[self.g, s - 1], r1.at[self.g, s - 1], at(*to))
            c.start()
            self.copies1.append(c)
        self.sent += self.copies1

    def piece(self, pos):
        b = pos[self.plane[0]] * 4 + pos[self.plane[1]]
        half = self.width // 2
        return (b // 2) * 16, (b % 2) * half, half

    def to_plane(self):
        s2, r2 = self.sems[4:6]
        for c in self.copies1:
            c.wait_recv()
        base = pl.multiple_of(self.here[self.axis] * 128, 128)

        def add(i, _):
            rows = rows_at(i, 16)
            total = self.h_sum[pl.ds(pl.multiple_of(base + i * 16, 16), 16), self.cols].astype(f32)
            for s in range(3):
                total = total + self.q_in[s, rows, :].astype(f32)
            self.q_sum[rows, :] = total.astype(bf16)
            return 0

        lax.fori_loop(0, 8, add, 0)
        self.copies2 = []
        for n, (s, t) in enumerate(plane_steps()):
            to = turned(turned(self.here, self.plane[0], s), self.plane[1], t)
            row, col, half = self.piece(to)
            src = self.q_sum.at[pl.ds(pl.multiple_of(row, 16), 16), pl.ds(pl.multiple_of(col, 128), half)]
            c = remote(src, self.f_in.at[n], s2.at[self.g, n], r2.at[self.g, n], at(*to))
            c.start()
            self.copies2.append(c)
        self.sent += self.copies2

    def from_plane(self):
        t2, u2 = self.sems[6:8]
        for c in self.copies2:
            c.wait_recv()
        row, col, half = self.piece(self.here)
        total = self.q_sum[pl.ds(pl.multiple_of(row, 16), 16), pl.ds(pl.multiple_of(col, 128), half)].astype(f32)
        for n in range(15):
            total = total + self.f_in[n].astype(f32)
        self.f_sum[...] = (total * self.scale).astype(bf16)
        spot = self.out.at[
            pl.ds(pl.multiple_of(self.keep + self.here[self.axis] * 128 + row, 16), 16),
            pl.ds(pl.multiple_of(self.col + col, 128), half),
        ]
        self.copies3 = []
        for n, (s, t) in enumerate(plane_steps()):
            to = turned(turned(self.here, self.plane[0], s), self.plane[1], t)
            c = remote(self.f_sum, spot, t2.at[self.g, n], u2.at[self.g, n], at(*to))
            c.start()
            self.copies3.append(c)
        self.own = pltpu.make_async_copy(self.f_sum, spot, t2.at[self.g, 15])
        self.own.start()
        self.sent += self.copies3

    def from_axis(self):
        t1, u1 = self.sems[8:10]
        self.own.wait()
        for c in self.copies3:
            c.wait_recv()
        spot = self.out.at[pl.ds(pl.multiple_of(self.keep + self.here[self.axis] * 128, 128), 128), self.cols]
        self.copies4 = []
        for s in (2, 1, 3):
            c = remote(spot, spot, t1.at[self.g, s - 1], u1.at[self.g, s - 1], at(*turned(self.here, self.axis, s)))
            c.start()
            self.copies4.append(c)
        self.sent += self.copies4

    def to_mate(self):
        t0, u0 = self.sems[10:12]
        for c in self.copies4:
            c.wait_recv()
        spot = self.out.at[pl.ds(self.keep, 512), self.cols]
        self.copy5 = remote(spot, spot, t0.at[self.g], u0.at[self.g], self.mate)
        self.copy5.start()

    def finish(self):
        self.copy5.wait()
        for c in self.sent:
            c.wait_send()


def spread_copies(pack_ref, got_ref, send, recv):
    here = coords()
    me = here[0] * 4 + here[1]
    copies = []
    for n, (s, t) in enumerate(plane_steps()):
        to = turned(turned(here, 0, s), 1, t)
        copies.append(remote(pack_ref.at[to[0] * 4 + to[1]], got_ref.at[me], send.at[n], recv.at[n], at(*to)))
    return copies, pltpu.make_async_copy(pack_ref.at[me], got_ref.at[me], send.at[15])


def mover():
    l = lax.broadcasted_iota(jnp.int32, (256, 256), 0)
    n = lax.broadcasted_iota(jnp.int32, (256, 256), 1)
    swapped = jnp.where((n >= 64) & (n < 128), n + 64, jnp.where((n >= 128) & (n < 192), n - 64, n))
    return (l == swapped).astype(bf16)


def main_kernel(
    scale, start_ref, len_ref, masked_ref, pack_ref, values_ref, part_ref, ext_ref, fine_ref, base_ref,
    density_ref, xt_ref, at_ref, out_ref,
    got, low, high, parts, lo, hi, weighted, bands, across, pack_a, got_a, x_rows, w, h_in, h_sum, *rest,
):
    q_in, q_sum, f_in, f_sum = rest[0:3], rest[3:6], rest[6:9], rest[9:12]
    sems = rest[12:24]
    sd, rd, sh, rh, sx, rx, sa, ra = rest[24:]
    here = coords()
    z, x, y, core = here
    orb, comp = lax.axis_index("orb"), lax.axis_index("comp")
    first_orbital, first_plane = orb * 64, comp * 16
    targets = [at(z, x, y, 1 - core), at(z, x, lax.rem(y + 3 + 2 * core, 4), 1 - core)]
    for a in (0, 1, 2):
        targets += [at(*turned(here, a, s)) for s in (1, 2, 3)]
    for a, b in ((0, 1), (0, 2), (1, 2)):
        targets += [at(*turned(turned(here, a, s), b, t)) for s in (1, 2, 3) for t in (1, 2, 3)]
    greet(targets)

    density_copies = []
    for n, (s, t) in enumerate(plane_steps()):
        to = turned(turned(here, 0, s), 1, t)
        density_copies.append(remote(part_ref, parts.at[n], sd.at[n], rd.at[n], at(*to)))
    halo_copies = [
        remote(masked_ref, low, sh.at[0], rh.at[0], {"orb": orb, "comp": lax.rem(comp + 1, 8)}),
        remote(masked_ref, high, sh.at[1], rh.at[1], {"orb": orb, "comp": lax.rem(comp + 7, 8)}),
    ]
    spread_x, own_x = spread_copies(pack_ref, got, sx, rx)
    spread_a, own_a = spread_copies(pack_a, got_a, sa, ra)
    for c in density_copies + halo_copies + spread_x + [own_x]:
        c.start()

    fine = fine_points(fine_ref) > 0.5

    def build(n, _):
        bands[n] = band(base_ref[pl.ds(n, 1), :])
        return 0

    lax.fori_loop(0, 16, build, 0, unroll=2)
    for e in range(4):
        bands[16 + e] = band(base_ref[pl.ds(20 + e, 1), :])
    spot = lax.rem(lax.broadcasted_iota(jnp.int32, (16, 256), 1), 48)
    edge = ((comp == 0) & (spot < 16)) | ((comp == 7) & (spot >= 32))
    for e in range(4):
        rolled = pltpu.roll(jnp.broadcast_to(base_ref[pl.ds(24 + e, 1), :], (16, 256)), 0, 1, stride=1, stride_axis=0)
        across[pl.ds(e * 16, 16), :] = jnp.where(edge, 0.0, rolled).astype(bf16)

    density = part_ref[...]
    for n in range(15):
        density_copies[n].wait_recv()
        density = density + parts[n]
    density_ref[...] = density
    potential = ext_ref[...] - xc_factor * jnp.exp(jnp.log(density) * (1.0 / 3.0))

    def weigh(o, _):
        weighted[o] = (potential * values_ref[o]).astype(bf16)
        return 0

    lax.fori_loop(0, 64, weigh, 0, unroll=4)

    def along(i, _):
        for e in range(4):
            total = jnp.dot(weighted[rows_at(i, 16)].reshape(256, 256), bands[16 + e], preferred_element_type=f32)
            for d in range(4):
                rows = masked_ref[rows_at(i, 16), d].reshape(256, 256)
                total = total + jnp.dot(rows, bands[d * 4 + e], preferred_element_type=f32)
            for n in range(16):
                rows = pl.ds(pl.multiple_of((i * 16 + n) * 64 + e * 16, 16), 16)
                lo[rows, :] = total[n * 16 : n * 16 + 16, :128]
                hi[rows, :] = total[n * 16 : n * 16 + 16, 128:]
        return 0

    lax.fori_loop(0, 4, along, 0)
    for c in halo_copies:
        c.wait_recv()

    def cross(o, _):
        window = jnp.concatenate([ref[o, d] for d in range(4) for ref in (low, masked_ref, high)], axis=0)
        summed = jnp.dot(across[:, :192], window, preferred_element_type=f32)
        inside = inside_planes(start_ref, len_ref, first_orbital, first_plane, o)
        for e in range(4):
            on = inside if e == 0 else inside & fine
            rows = pl.ds(pl.multiple_of(o * 64 + e * 16, 16), 16)
            part = summed[e * 16 : e * 16 + 16]
            lo[rows, :] = jnp.where(on[:, :128], part[:, :128] + lo[rows, :], 0.0)
            hi[rows, :] = jnp.where(on[:, 128:], part[:, 128:] + hi[rows, :], 0.0)
        return 0

    lax.fori_loop(0, 64, cross, 0, unroll=4)
    pack(lo, hi, pack_a)
    for c in spread_a + [own_a]:
        c.start()

    move = mover()
    own_x.wait()
    for c in spread_x:
        c.wait_recv()

    def unpack_x(m, _):
        pair = jnp.concatenate([got[2 * m], got[2 * m + 1]], axis=1)
        turned_back = jnp.dot(pair, move, preferred_element_type=f32).astype(bf16)
        lanes = pl.ds(pl.multiple_of(128 * m, 128), 128)
        xt_ref[0:512, lanes] = turned_back[:, :128]
        xt_ref[512:1024, lanes] = turned_back[:, 128:]
        rows = lax.dot_general(move, pair, (((1,), (1,)), ((), ())), preferred_element_type=f32).astype(bf16)
        x_rows[lanes, 0:512] = rows[:128]
        x_rows[lanes, 512:1024] = rows[128:]
        return 0

    lax.fori_loop(0, 8, unpack_x, 0)
    groups = [
        Group(g, scale, w, out_ref, h_in, h_sum, q_in[g], q_sum[g], f_in[g], f_sum[g], sems) for g in range(3)
    ]
    overlap, first, second = groups

    def overlaps(i, _):
        rows = rows_at(i, 128)
        w[rows, 0:1024] = jnp.dot(x_rows[rows, :], xt_ref[...], preferred_element_type=f32).astype(bf16)
        return 0

    lax.fori_loop(0, 8, overlaps, 0)
    overlap.begin()
    overlap.to_axis()
    overlap.to_plane()
    own_a.wait()
    for c in spread_a:
        c.wait_recv()

    def unpack_a(m, _):
        pair = jnp.concatenate([got_a[2 * m], got_a[2 * m + 1]], axis=1)
        turned_back = jnp.dot(pair, move, preferred_element_type=f32).astype(bf16)
        lanes = pl.ds(pl.multiple_of(128 * m, 128), 128)
        at_ref[0:512, lanes] = turned_back[:, :128]
        at_ref[512:1024, lanes] = turned_back[:, 128:]
        return 0

    lax.fori_loop(0, 8, unpack_a, 0)

    def multipliers(i, _):
        rows = rows_at(i, 128)
        w[rows, 1024:2048] = jnp.dot(x_rows[rows, :], at_ref[...], preferred_element_type=f32).astype(bf16)
        return 0

    lax.fori_loop(0, 8, multipliers, 0)
    first.begin()
    second.begin()
    overlap.from_plane()
    first.to_axis()
    second.to_axis()
    overlap.from_axis()
    first.to_plane()
    second.to_plane()
    first.from_plane()
    second.from_plane()
    first.from_axis()
    second.from_axis()
    overlap.to_mate()
    first.to_mate()
    second.to_mate()
    for c in density_copies + halo_copies + spread_x + spread_a:
        c.wait_send()
    for group in groups:
        group.finish()


def main_step(scale, start, length, masked, packed, values, part, external, fine, base):
    dma = pltpu.SemaphoreType.DMA
    vm = pltpu.VMEM
    widths = [g[1] for g in GROUPS]
    spread_buffer = vm((16, 512, 128), bf16)
    square = (1024, 1024)
    return pl.pallas_call(
        functools.partial(main_kernel, scale),
        out_shape=(shape((16, 256), f32), shape(square), shape(square), shape((1024, 2048))),
        in_specs=[SM, SM] + [VM] * 7,
        out_specs=(VM,) * 4,
        scratch_shapes=[spread_buffer, vm(masked.shape, bf16), vm(masked.shape, bf16), vm((15, 16, 256), f32)]
        + [vm((4096, 128), f32)] * 2
        + [vm((64, 16, 256), bf16), vm((20, 256, 256), bf16), vm((64, 256), bf16), spread_buffer, spread_buffer]
        + [vm(square, bf16), vm((1024, 2048), bf16), vm((512, 2048), bf16), vm((512, 2048), bf16)]
        + [vm((3, 128, n), bf16) for n in widths]
        + [vm((128, n), bf16) for n in widths]
        + [vm((15, 16, n // 2), bf16) for n in widths]
        + [vm((16, n // 2), bf16) for n in widths]
        + [dma((3,)), dma((3,)), dma((3, 3)), dma((3, 3)), dma((3, 15)), dma((3, 15))]
        + [dma((3, 16)), dma((3, 15)), dma((3, 3)), dma((3, 3)), dma((3,)), dma((3,))]
        + [dma((15,)), dma((15,)), dma((2,)), dma((2,)), dma((16,)), dma((15,)), dma((16,)), dma((15,))],
        compiler_params=pltpu.CompilerParams(collective_id=3, has_side_effects=True, vmem_limit_bytes=VMEM_MAIN),
        name="main",
    )(start, length, masked, packed, values, part, external, fine, base)


VMEM_MAIN = 52 << 20

def filter_rows(kinetic_taps, magic_taps):
    def ring(rows, before):
        rows = jnp.pad(rows, ((0, 0), (0, 256 - rows.shape[1])))
        return jnp.roll(rows, -before, axis=1)

    taps = jnp.transpose(kinetic_taps.astype(f32), (2, 1, 0))
    magic = jnp.transpose(magic_taps.astype(f32))
    across = jnp.pad(jnp.transpose(kinetic_taps.astype(f32), (1, 2, 0)), ((0, 0), (0, 0), (2, 17))).reshape(4, 192)
    return jnp.concatenate(
        [
            ring(taps.reshape(16, 29)[:, ::-1], 14),
            ring(magic[:, ::-1], 8),
            ring(magic, 7),
            jnp.pad(across, ((0, 0), (0, 64))),
        ],
        axis=0,
    )


def local(psi, region_start, region_len, fine_mask, occupation, kinetic_taps, magic_taps, external):
    base = filter_rows(kinetic_taps, magic_taps)
    masked, packed, values, part = first_step(region_start, region_len, occupation, psi, fine_mask, base)
    density, masked_k, applied_k, both = main_step(
        1.0 / 32768, region_start, region_len, masked, packed, values, part, external, fine_mask, base
    )
    density = lax.dynamic_slice_in_dim(density, lax.axis_index("orb") * 16, 16, 1)
    intersection_round, lagrange_round = both[:, :1024], both[:, 1024:]
    gradient = applied_k.astype(f32) - jnp.dot(masked_k, lagrange_round, preferred_element_type=f32)
    trial = (masked_k.astype(f32) - step_length * gradient).astype(bf16)
    following = 1.5 * trial.astype(f32) - 0.5 * jnp.dot(trial, intersection_round, preferred_element_type=f32)
    psi_next = jnp.transpose(following.astype(bf16).reshape(4, 16, 16, 1024), (3, 0, 1, 2))
    return (density, psi_next)


def solution(mesh):
    return jax.shard_map(
        local,
        mesh=mesh,
        in_specs=(
            P("orb", None, "comp", None),
            P(),
            P(),
            P("comp", None),
            P(),
            P(),
            P(),
            P("comp", None),
        ),
        out_specs=(P("comp", "orb"), P(None, None, "comp", "orb")),
        check_vma=False,
    )
```

```python
import functools

import jax
import jax.numpy as jnp
from jax import lax
from jax.experimental import pallas as pl
from jax.experimental.pallas import tpu as pltpu
from jax.sharding import PartitionSpec as P

ZB = 16
xc_factor = 0.98474502
step_length = 0.1
f32, bf16 = jnp.float32, jnp.bfloat16

MESH = pl.DeviceIdType.MESH


def coords():
    orb, comp = lax.axis_index("orb"), lax.axis_index("comp")
    return orb // 4, orb % 4, comp // 2, comp % 2


def at(z, x, y, core):
    return {"orb": z * 4 + x, "comp": y * 2 + core}


def turned(pos, axis, step):
    pos = list(pos)
    pos[axis] = lax.rem(pos[axis] + step, 4)
    return tuple(pos)


def rows_at(i, size):
    return pl.ds(pl.multiple_of(i * size, size), size)


def eye(n):
    return (
        lax.broadcasted_iota(jnp.int32, (n, n), 0) == lax.broadcasted_iota(jnp.int32, (n, n), 1)
    ).astype(bf16)


def band(row):
    wide = jnp.broadcast_to(row, (256, 256))
    rolled = pltpu.roll(wide, 0, 1, stride=1, stride_axis=0)
    gap = lax.broadcasted_iota(jnp.int32, (256, 256), 0) - lax.broadcasted_iota(jnp.int32, (256, 256), 1)
    return jnp.where((gap <= 14) & (gap >= -14), rolled, 0.0).astype(bf16)


def inside_planes(start_ref, len_ref, first_orbital, first_plane, o, width):
    begin = start_ref[first_orbital + o] - first_plane
    plane = lax.broadcasted_iota(jnp.int32, (16, width), 0)
    return (plane >= begin) & (plane < begin + len_ref[first_orbital + o])


def fine_points(fine):
    spread = (
        lax.broadcasted_iota(jnp.int32, (16, 256), 1) // ZB == lax.broadcasted_iota(jnp.int32, (16, 256), 0)
    ).astype(bf16)
    return jnp.dot((fine > 0).astype(f32).astype(bf16), spread, preferred_element_type=f32)


def placed(rows, spot):
    taps = rows.shape[1]
    t = lax.broadcasted_iota(jnp.int32, (taps, 256), 0)
    lane = lax.broadcasted_iota(jnp.int32, (taps, 256), 1)
    return jnp.dot(rows, (lane == spot(t)).astype(bf16), preferred_element_type=f32)


def pack(wide, pack_ref, half):
    unit = eye(128)

    def step(j, _):
        row = half * 4096 + j
        both = jnp.concatenate([wide[pl.ds(row, 64, stride=64), :], wide[pl.ds(row + 32, 64, stride=64), :]], axis=0)
        turned_over = lax.dot_general(
            unit, both.astype(bf16), (((1,), (1,)), ((), ())), preferred_element_type=f32
        ).astype(bf16)
        for q in range(8):
            pack_ref[half * 8 + q, rows_at(j, 16), :] = turned_over[q * 16 : q * 16 + 16, :]
        return 0

    lax.fori_loop(0, 32, step, 0, unroll=4)


VM = pl.BlockSpec(memory_space=pltpu.VMEM)
HB = pl.BlockSpec(memory_space=pl.ANY)


def shape(dims, kind=bf16):
    return jax.ShapeDtypeStruct(dims, kind)


def plane_steps():
    return [(s, t) for s in range(4) for t in range(4) if s or t]


FAR_FIRST = (
    (2, 2), (0, 2), (2, 0), (1, 2), (3, 2), (2, 1), (2, 3), (1, 1), (3, 3), (3, 1), (1, 3), (0, 1), (0, 3), (1, 0), (3, 0),
)


GROUPS = ((0, 1024, 2, (0, 1)), (1024, 512, 1, (0, 2)), (1536, 512, 0, (1, 2)))


def remote(src, dst, ssem, rsem, to):
    return pltpu.make_async_remote_copy(
        src_ref=src, dst_ref=dst, send_sem=ssem, recv_sem=rsem, device_id=to, device_id_type=MESH
    )


class Group:
    def __init__(self, g, scale, w_ref, out_ref, h_in, h_sum, q_in, q_sum, f_in, f_sum, sems):
        self.g, self.scale = g, scale
        self.w, self.out, self.h_in, self.h_sum = w_ref, out_ref, h_in, h_sum
        self.q_in, self.q_sum, self.f_in, self.f_sum = q_in, q_sum, f_in, f_sum
        self.sems = sems
        self.col, self.width, self.axis, self.plane = GROUPS[g]
        self.cols = pl.ds(self.col, self.width)
        self.here = coords()
        z, x, y, core = self.here
        self.mate = at(z, x, y, 1 - core)
        self.keep = pl.multiple_of(core * 512, 512)
        self.give = pl.multiple_of(512 - core * 512, 512)
        self.sent = []

    def begin(self):
        s0, r0 = self.sems[0:2]
        rows = pl.ds(self.give, 512)
        self.copy0 = remote(self.w.at[rows, self.cols], self.h_in.at[:, self.cols], s0.at[self.g], r0.at[self.g], self.mate)
        self.copy0.start()

    def to_axis(self):
        s1, r1 = self.sems[2:4]
        self.copy0.wait()

        def add(i, _):
            rows = rows_at(i, 32)
            mine = pl.ds(pl.multiple_of(self.keep + i * 32, 32), 32)
            total = self.w[mine, self.cols].astype(f32) + self.h_in[rows, self.cols].astype(f32)
            self.h_sum[rows, self.cols] = total.astype(bf16)
            return 0

        lax.fori_loop(0, 16, add, 0)
        self.copies1 = []
        for s in (2, 1, 3):
            to = turned(self.here, self.axis, s)
            rows = pl.ds(pl.multiple_of(to[self.axis] * 128, 128), 128)
            c = remote(self.h_sum.at[rows, self.cols], self.q_in.at[s - 1], s1.at[self.g, s - 1], r1.at[self.g, s - 1], at(*to))
            c.start()
            self.copies1.append(c)
        self.sent += self.copies1

    def piece(self, pos):
        b = pos[self.plane[0]] * 4 + pos[self.plane[1]]
        half = self.width // 2
        return (b // 2) * 16, (b % 2) * half, half

    def to_plane(self):
        s2, r2 = self.sems[4:6]
        for c in self.copies1:
            c.wait_recv()
        base = pl.multiple_of(self.here[self.axis] * 128, 128)

        def add(i, _):
            rows = rows_at(i, 16)
            total = self.h_sum[pl.ds(pl.multiple_of(base + i * 16, 16), 16), self.cols].astype(f32)
            for s in range(3):
                total = total + self.q_in[s, rows, :].astype(f32)
            self.q_sum[rows, :] = total.astype(bf16)
            return 0

        lax.fori_loop(0, 8, add, 0)
        self.copies2 = []
        for n, (s, t) in enumerate(plane_steps()):
            to = turned(turned(self.here, self.plane[0], s), self.plane[1], t)
            row, col, half = self.piece(to)
            src = self.q_sum.at[pl.ds(pl.multiple_of(row, 16), 16), pl.ds(pl.multiple_of(col, 128), half)]
            c = remote(src, self.f_in.at[n], s2.at[self.g, n], r2.at[self.g, n], at(*to))
            c.start()
            self.copies2.append(c)
        self.sent += self.copies2

    def from_plane(self):
        t2, u2 = self.sems[6:8]
        for c in self.copies2:
            c.wait_recv()
        row, col, half = self.piece(self.here)
        total = self.q_sum[pl.ds(pl.multiple_of(row, 16), 16), pl.ds(pl.multiple_of(col, 128), half)].astype(f32)
        for n in range(15):
            total = total + self.f_in[n].astype(f32)
        self.f_sum[...] = (total * self.scale).astype(bf16)
        spot = self.out.at[
            pl.ds(pl.multiple_of(self.keep + self.here[self.axis] * 128 + row, 16), 16),
            pl.ds(pl.multiple_of(self.col + col, 128), half),
        ]
        self.copies3 = []
        for n, (s, t) in enumerate(plane_steps()):
            to = turned(turned(self.here, self.plane[0], s), self.plane[1], t)
            c = remote(self.f_sum, spot, t2.at[self.g, n], u2.at[self.g, n], at(*to))
            c.start()
            self.copies3.append(c)
        self.own = pltpu.make_async_copy(self.f_sum, spot, t2.at[self.g, 15])
        self.own.start()
        self.sent += self.copies3

    def from_axis(self):
        t1, u1 = self.sems[8:10]
        self.own.wait()
        for c in self.copies3:
            c.wait_recv()
        spot = self.out.at[pl.ds(pl.multiple_of(self.keep + self.here[self.axis] * 128, 128), 128), self.cols]
        self.copies4 = []
        for s in (2, 1, 3):
            c = remote(spot, spot, t1.at[self.g, s - 1], u1.at[self.g, s - 1], at(*turned(self.here, self.axis, s)))
            c.start()
            self.copies4.append(c)
        self.sent += self.copies4

    def to_mate(self):
        t0, u0 = self.sems[10:12]
        for c in self.copies4:
            c.wait_recv()
        spot = self.out.at[pl.ds(self.keep, 512), self.cols]
        self.copy5 = remote(spot, spot, t0.at[self.g], u0.at[self.g], self.mate)
        self.copy5.start()

    def finish(self):
        self.copy5.wait()
        for c in self.sent:
            c.wait_send()


def spread_copies(pack_ref, got_ref, send, recv):
    here = coords()
    me = here[0] * 4 + here[1]
    copies = []
    for n, (s, t) in enumerate(FAR_FIRST):
        to = turned(turned(here, 0, s), 1, t)
        copies.append((to[0], remote(pack_ref.at[to[0] * 4 + to[1]], got_ref.at[me], send.at[n], recv.at[n], at(*to))))
    return copies, (here[0], pltpu.make_async_copy(pack_ref.at[me], got_ref.at[me], send.at[15]))


def started(copy, chosen):
    @pl.when(chosen)
    def _():
        copy.start()


def mover():
    l = lax.broadcasted_iota(jnp.int32, (256, 256), 0)
    n = lax.broadcasted_iota(jnp.int32, (256, 256), 1)
    swapped = jnp.where((n >= 64) & (n < 128), n + 64, jnp.where((n >= 128) & (n < 192), n - 64, n))
    return (l == swapped).astype(bf16)


def main_kernel(
    scale, psi_hbm, start_hbm, len_hbm, fine_hbm, occ_hbm, taps_hbm, magic_hbm, ext_hbm, density_ref, trial_hbm, s_hbm,
    psi, start_ref, len_ref, fine_ref, occ_ref, taps, magic, ext_ref, sem_in, sem_psi,
    masked, values, part, pack_x, got, low, high, parts, wide, fine_on, weighted, bands, forward, across, pack_a, got_a,
    xt, a_t, trial, out, x_rows, w, h_in, h_sum, *rest,
):
    q_in, q_sum, f_in, f_sum = rest[0:3], rest[3:6], rest[6:9], rest[9:12]
    sems = rest[12:24]
    sd, rd, sh, rh, sx, rx, sa, ra, sem_out = rest[24:]
    here = coords()
    z, x, y, core = here
    orb, comp = lax.axis_index("orb"), lax.axis_index("comp")
    first_orbital, first_plane = orb * 64, comp * 16

    small = [
        pltpu.make_async_copy(src, dst, sem_in.at[n])
        for n, (src, dst) in enumerate(
            (
                (taps_hbm, taps), (magic_hbm, magic), (start_hbm, start_ref), (len_hbm, len_ref), (fine_hbm, fine_ref),
                (occ_hbm, occ_ref), (ext_hbm, ext_ref),
            )
        )
    ]
    for c in small:
        c.start()
    psi_copies = [
        pltpu.make_async_copy(psi_hbm.at[pl.ds(16 * n, 16)], psi.at[pl.ds(16 * n, 16)], sem_psi.at[n]) for n in range(4)
    ]
    for c in psi_copies:
        c.start()

    targets = [at(z, x, y, 1 - core), at(z, x, lax.rem(y + 3 + 2 * core, 4), 1 - core)]
    for a in (0, 1, 2):
        targets += [at(*turned(here, a, s)) for s in (1, 2, 3)]
    for a, b in ((0, 1), (0, 2), (1, 2)):
        targets += [at(*turned(turned(here, a, s), b, t)) for s in (1, 2, 3) for t in (1, 2, 3)]
    barrier = pltpu.get_barrier_semaphore()
    for t in targets:
        pl.semaphore_signal(barrier, inc=1, device_id=t, device_id_type=MESH)

    for c in small:
        c.wait()
    rows = []
    for e in range(4):
        rows.append(placed(taps[e], lambda t: lax.rem(270 - t, 256)))
    magic_rows = placed(magic[...], lambda t: lax.rem(263 - t, 256))
    adjoint_rows = placed(magic[...], lambda t: lax.rem(t + 249, 256))
    for d in range(4):
        for e in range(4):
            bands[d * 4 + e] = band(rows[e][d : d + 1])
        bands[16 + d] = band(adjoint_rows[d : d + 1])
        forward[d] = band(magic_rows[d : d + 1])
    spot = lax.rem(lax.broadcasted_iota(jnp.int32, (16, 256), 1), 48)
    edge = ((comp == 0) & (spot < 16)) | ((comp == 7) & (spot >= 32))
    for e in range(4):
        line = sum(placed(taps[e, d : d + 1], lambda t, d=d: t + (d * 48 + 2)) for d in range(4))
        rolled = pltpu.roll(jnp.broadcast_to(line, (16, 256)), 0, 1, stride=1, stride_axis=0)
        across[pl.ds(e * 16, 16), :] = jnp.where(edge, 0.0, rolled).astype(bf16)

    fine_on[...] = fine_points(fine_ref[...])
    fine = fine_on[...] > 0.5
    for n in range(4):
        psi_copies[n].wait()

        def mask(o, _):
            inside = inside_planes(start_ref, len_ref, first_orbital, first_plane, o, 256)
            for c in range(4):
                on = inside if c == 0 else inside & fine
                value = jnp.where(on, psi[o, c].astype(f32), 0.0)
                masked[o, c] = value.astype(bf16)
                spots = pl.ds(pl.multiple_of(o * 64 + c * 16, 16), 16)
                wide[spots, :] = value[:, :128]
                wide[pl.ds(pl.multiple_of(4096 + o * 64 + c * 16, 16), 16), :] = value[:, 128:]
            return 0

        lax.fori_loop(16 * n, 16 * n + 16, mask, 0, unroll=2)
    def block(i, total):
        seen = jnp.zeros((256, 256), f32)
        for d in range(4):
            seen = seen + jnp.dot(masked[rows_at(i, 16), d].reshape(256, 256), forward[d], preferred_element_type=f32)
        for n in range(16):
            one = seen[n * 16 : n * 16 + 16]
            values[i * 16 + n] = one
            total = total + occ_ref[first_orbital + i * 16 + n].astype(f32) * (one * one)
        return total

    part[...] = lax.fori_loop(0, 4, block, jnp.zeros((16, 256), f32))
    halves = (lax.rem(x, 2), 1 - lax.rem(x, 2))
    spread_x, own_x = spread_copies(pack_x, got, sx, rx)
    spread_a, own_a = spread_copies(pack_a, got_a, sa, ra)
    pack(wide, pack_x, halves[0])
    pl.semaphore_wait(barrier, len(targets))

    halo_copies = []
    for n, h in enumerate(halves):
        lanes = pl.ds(pl.multiple_of(128 * h, 128), 128)
        source = masked.at[:, :, :, lanes]
        for k, (ref, turn) in enumerate(((low, 1), (high, 7))):
            halo_copies.append(
                remote(
                    source, ref.at[:, :, :, lanes], sh.at[2 * n + k], rh.at[2 * n + k],
                    {"orb": orb, "comp": lax.rem(comp + turn, 8)},
                )
            )
    for c in halo_copies:
        c.start()

    density_copies = []
    for n, (s, t) in enumerate(FAR_FIRST):
        to = turned(turned(here, 0, s), 1, t)
        density_copies.append(remote(part, parts.at[n], sd.at[n], rd.at[n], at(*to)))
    for c in density_copies:
        c.start()

    for to_z, c in spread_x + [own_x]:
        started(c, lax.div(to_z, 2) == halves[0])
    pack(wide, pack_x, halves[1])
    for to_z, c in spread_x + [own_x]:
        started(c, lax.div(to_z, 2) == halves[1])

    density = part[...]
    for n in range(15):
        density_copies[n].wait_recv()
        density = density + parts[n]
    density_ref[...] = pltpu.roll(density, 256 - orb * 16, 1)[:, :16]
    potential = ext_ref[...] - xc_factor * jnp.exp(jnp.log(density) * (1.0 / 3.0))

    def weigh(o, _):
        weighted[o] = (potential * values[o]).astype(bf16)
        return 0

    lax.fori_loop(0, 64, weigh, 0, unroll=4)

    def along(i, _):
        for e in range(4):
            total = jnp.dot(weighted[rows_at(i, 16)].reshape(256, 256), bands[16 + e], preferred_element_type=f32)
            for d in range(4):
                total = total + jnp.dot(
                    masked[rows_at(i, 16), d].reshape(256, 256), bands[d * 4 + e], preferred_element_type=f32
                )
            for n in range(16):
                spots = pl.ds(pl.multiple_of((i * 16 + n) * 64 + e * 16, 16), 16)
                wide[spots, :] = total[n * 16 : n * 16 + 16, :128]
                spots = pl.ds(pl.multiple_of(4096 + (i * 16 + n) * 64 + e * 16, 16), 16)
                wide[spots, :] = total[n * 16 : n * 16 + 16, 128:]
        return 0

    lax.fori_loop(0, 4, along, 0)

    for n, h in enumerate(halves):
        for c in halo_copies[2 * n : 2 * n + 2]:
            c.wait_recv()
        lanes = pl.ds(pl.multiple_of(128 * h, 128), 128)
        fine_half = fine_on[:, lanes] > 0.5

        def cross(i, _, h=h, lanes=lanes, fine_half=fine_half):
            o = 2 * i
            window = jnp.concatenate(
                [
                    jnp.concatenate([ref[o, d, :, lanes], ref[o + 1, d, :, lanes]], axis=1)
                    for d in range(4)
                    for ref in (low, masked, high)
                ],
                axis=0,
            )
            summed = jnp.dot(across[:, :192], window, preferred_element_type=f32)
            for k in range(2):
                inside = inside_planes(start_ref, len_ref, first_orbital, first_plane, o + k, 128)
                for e in range(4):
                    on = inside if e == 0 else inside & fine_half
                    spots = pl.ds(pl.multiple_of(h * 4096 + (o + k) * 64 + e * 16, 16), 16)
                    term = summed[e * 16 : e * 16 + 16, 128 * k : 128 * k + 128]
                    wide[spots, :] = jnp.where(on, term + wide[spots, :], 0.0)
            return 0

        lax.fori_loop(0, 32, cross, 0, unroll=4)
        pack(wide, pack_a, h)
        for to_z, c in spread_a + [own_a]:
            started(c, lax.div(to_z, 2) == h)

    move = mover()
    own_x[1].wait()
    for _, c in spread_x:
        c.wait_recv()

    def unpack_x(m, _):
        pair = jnp.concatenate([got[2 * m], got[2 * m + 1]], axis=1)
        turned_back = jnp.dot(pair, move, preferred_element_type=f32).astype(bf16)
        spots = pl.ds(pl.multiple_of(128 * m, 128), 128)
        xt[0:512, spots] = turned_back[:, :128]
        xt[512:1024, spots] = turned_back[:, 128:]
        across_rows = lax.dot_general(move, pair, (((1,), (1,)), ((), ())), preferred_element_type=f32).astype(bf16)
        x_rows[spots, 0:512] = across_rows[:128]
        x_rows[spots, 512:1024] = across_rows[128:]
        return 0

    lax.fori_loop(0, 8, unpack_x, 0)
    groups = [Group(g, scale, w, out, h_in, h_sum, q_in[g], q_sum[g], f_in[g], f_sum[g], sems) for g in range(3)]
    overlap, first, second = groups

    keep, give = pl.multiple_of(core * 512, 512), pl.multiple_of(512 - core * 512, 512)

    def products(other, col, first_row):
        def step(i, _):
            spots = pl.ds(pl.multiple_of(first_row + i * 256, 256), 256)
            w[spots, col : col + 1024] = jnp.dot(x_rows[spots, :], other[...], preferred_element_type=f32).astype(bf16)
            return 0

        lax.fori_loop(0, 2, step, 0)

    products(xt, 0, give)
    overlap.begin()
    products(xt, 0, keep)
    overlap.to_axis()
    overlap.to_plane()
    own_a[1].wait()
    for _, c in spread_a:
        c.wait_recv()

    def unpack_a(m, _):
        pair = jnp.concatenate([got_a[2 * m], got_a[2 * m + 1]], axis=1)
        turned_back = jnp.dot(pair, move, preferred_element_type=f32).astype(bf16)
        spots = pl.ds(pl.multiple_of(128 * m, 128), 128)
        a_t[0:512, spots] = turned_back[:, :128]
        a_t[512:1024, spots] = turned_back[:, 128:]
        return 0

    lax.fori_loop(0, 8, unpack_a, 0)
    products(a_t, 1024, give)
    first.begin()
    second.begin()
    products(a_t, 1024, keep)
    first.to_axis()
    second.to_axis()
    first.to_plane()
    second.to_plane()
    overlap.from_plane()
    first.from_plane()
    second.from_plane()
    first.from_axis()
    second.from_axis()
    overlap.from_axis()
    first.to_mate()
    second.to_mate()
    first.finish()
    second.finish()
    for n in range(4):
        spots = pl.ds(256 * n, 256)
        mine = xt[spots, :]
        gradient = a_t[spots, :].astype(f32) - jnp.dot(mine, out[:, 1024:2048], preferred_element_type=f32)
        trial[spots, :] = (mine.astype(f32) - step_length * gradient).astype(bf16)
    trial_copy = pltpu.make_async_copy(trial, trial_hbm, sem_out.at[0])
    trial_copy.start()
    overlap.to_mate()
    for c in density_copies + halo_copies + [c for _, c in spread_x + spread_a]:
        c.wait_send()
    overlap.finish()
    s_copy = pltpu.make_async_copy(out.at[:, pl.ds(0, 1024)], s_hbm, sem_out.at[1])
    s_copy.start()
    trial_copy.wait()
    s_copy.wait()


def last_kernel(trial_hbm, s_hbm, part_hbm, next_hbm, density_hbm, trial, s_all, part, following, sems):
    copies = [pltpu.make_async_copy(s_hbm, s_all, sems.at[0])]
    for n in range(4):
        rows = pl.ds(256 * n, 256)
        copies.append(pltpu.make_async_copy(trial_hbm.at[rows], trial.at[rows], sems.at[1 + n]))
    copies.append(pltpu.make_async_copy(part_hbm, part, sems.at[5]))
    for c in copies:
        c.start()
    copies[5].wait()
    done = [pltpu.make_async_copy(part, density_hbm, sems.at[6])]
    done[0].start()
    copies[0].wait()
    for n in range(4):
        rows = pl.ds(256 * n, 256)
        copies[1 + n].wait()
        now = trial[rows, :]
        stepped = 1.5 * now.astype(f32) - 0.5 * jnp.dot(now, s_all[...], preferred_element_type=f32)
        following[rows, :] = stepped.astype(bf16)
        done.append(pltpu.make_async_copy(following.at[rows], next_hbm.at[rows], sems.at[7 + n]))
        done[-1].start()
    for c in done:
        c.wait()


def last_step(trial, s_all, part):
    vm = pltpu.VMEM
    square = vm((1024, 1024), bf16)
    return pl.pallas_call(
        last_kernel,
        out_shape=(shape((1024, 1024)), shape((16, 16), f32)),
        in_specs=[HB] * 3,
        out_specs=(HB,) * 2,
        scratch_shapes=[square, square, vm((16, 16), f32), square, pltpu.SemaphoreType.DMA((11,))],
        compiler_params=pltpu.CompilerParams(vmem_limit_bytes=VMEM_MAIN),
        name="last",
    )(trial, s_all, part)


def main_step(scale, *args):
    dma = pltpu.SemaphoreType.DMA
    vm = pltpu.VMEM
    sm = pltpu.SMEM
    widths = [g[1] for g in GROUPS]
    spread_buffer = vm((16, 512, 128), bf16)
    square = vm((1024, 1024), bf16)
    orbitals = vm((64, 4, 16, 256), bf16)
    return pl.pallas_call(
        functools.partial(main_kernel, scale),
        out_shape=(shape((16, 16), f32), shape((1024, 1024)), shape((1024, 1024))),
        in_specs=[HB] * 8,
        out_specs=(VM, HB, HB),
        scratch_shapes=[orbitals, sm((1024,), jnp.int32), sm((1024,), jnp.int32), vm((16, 16), jnp.int32)]
        + [sm((1024,), jnp.int32), vm((4, 4, 29), bf16), vm((4, 16), bf16), vm((16, 256), f32), dma((7,)), dma((4,))]
        + [orbitals, vm((64, 16, 256), f32), vm((16, 256), f32), spread_buffer, spread_buffer, orbitals, orbitals]
        + [vm((15, 16, 256), f32), vm((8192, 128), f32), vm((16, 256), f32), vm((64, 16, 256), bf16)]
        + [vm((20, 256, 256), bf16), vm((4, 256, 256), bf16), vm((64, 256), bf16), spread_buffer, spread_buffer]
        + [square, square, square, vm((1024, 2048), bf16), square]
        + [vm((1024, 2048), bf16), vm((512, 2048), bf16), vm((512, 2048), bf16)]
        + [vm((3, 128, n), bf16) for n in widths]
        + [vm((128, n), bf16) for n in widths]
        + [vm((15, 16, n // 2), bf16) for n in widths]
        + [vm((16, n // 2), bf16) for n in widths]
        + [dma((3,)), dma((3,)), dma((3, 3)), dma((3, 3)), dma((3, 15)), dma((3, 15))]
        + [dma((3, 16)), dma((3, 15)), dma((3, 3)), dma((3, 3)), dma((3,)), dma((3,))]
        + [dma((15,)), dma((15,)), dma((4,)), dma((4,)), dma((16,)), dma((15,)), dma((16,)), dma((15,)), dma((2,))],
        compiler_params=pltpu.CompilerParams(collective_id=3, has_side_effects=True, vmem_limit_bytes=VMEM_MAIN),
        name="main",
    )(*args)


VMEM_MAIN = 58 << 20


def local(psi, region_start, region_len, fine_mask, occupation, kinetic_taps, magic_taps, external):
    density, trial, intersection = main_step(
        1.0 / 32768, psi, region_start, region_len, fine_mask, occupation,
        jnp.transpose(kinetic_taps, (1, 2, 0)), jnp.transpose(magic_taps), external,
    )
    following, density = last_step(trial, intersection, density)
    return (density, jnp.transpose(following.reshape(4, 16, 16, 1024), (3, 0, 1, 2)))


def solution(mesh):
    return jax.shard_map(
        local,
        mesh=mesh,
        in_specs=(
            P("orb", None, "comp", None),
            P(),
            P(),
            P("comp", None),
            P(),
            P(),
            P(),
            P("comp", None),
        ),
        out_specs=(P("comp", "orb"), P(None, None, "comp", "orb")),
        check_vma=False,
    )
```

```python
import functools

import jax
import jax.numpy as jnp
from jax import lax
from jax.experimental import pallas as pl
from jax.experimental.pallas import tpu as pltpu
from jax.sharding import PartitionSpec as P

ZB = 16
xc_factor = 0.98474502
step_length = 0.1
f32, bf16 = jnp.float32, jnp.bfloat16

MESH = pl.DeviceIdType.MESH


def coords():
    orb, comp = lax.axis_index("orb"), lax.axis_index("comp")
    return orb // 4, orb % 4, comp // 2, comp % 2


def at(z, x, y, core):
    return {"orb": z * 4 + x, "comp": y * 2 + core}


def turned(pos, axis, step):
    pos = list(pos)
    pos[axis] = lax.rem(pos[axis] + step, 4)
    return tuple(pos)


def rows_at(i, size):
    return pl.ds(pl.multiple_of(i * size, size), size)


def eye(n):
    return (
        lax.broadcasted_iota(jnp.int32, (n, n), 0) == lax.broadcasted_iota(jnp.int32, (n, n), 1)
    ).astype(bf16)


def band(row):
    wide = jnp.broadcast_to(row, (256, 256))
    rolled = pltpu.roll(wide, 0, 1, stride=1, stride_axis=0)
    gap = lax.broadcasted_iota(jnp.int32, (256, 256), 0) - lax.broadcasted_iota(jnp.int32, (256, 256), 1)
    return jnp.where((gap <= 14) & (gap >= -14), rolled, 0.0).astype(bf16)


def inside_planes(start_ref, len_ref, first_orbital, first_plane, o, width):
    begin = start_ref[first_orbital + o] - first_plane
    plane = lax.broadcasted_iota(jnp.int32, (16, width), 0)
    return (plane >= begin) & (plane < begin + len_ref[first_orbital + o])


def fine_points(fine):
    spread = (
        lax.broadcasted_iota(jnp.int32, (16, 256), 1) // ZB == lax.broadcasted_iota(jnp.int32, (16, 256), 0)
    ).astype(bf16)
    return jnp.dot((fine > 0).astype(f32).astype(bf16), spread, preferred_element_type=f32)


def placed(rows, spot):
    taps = rows.shape[1]
    t = lax.broadcasted_iota(jnp.int32, (taps, 256), 0)
    lane = lax.broadcasted_iota(jnp.int32, (taps, 256), 1)
    return jnp.dot(rows, (lane == spot(t)).astype(bf16), preferred_element_type=f32)


def pack(wide, pack_ref, half):
    unit = eye(128)

    def step(j, _):
        row = half * 4096 + j
        both = jnp.concatenate([wide[pl.ds(row, 64, stride=64), :], wide[pl.ds(row + 32, 64, stride=64), :]], axis=0)
        turned_over = lax.dot_general(
            unit, both.astype(bf16), (((1,), (1,)), ((), ())), preferred_element_type=f32
        ).astype(bf16)
        for q in range(8):
            pack_ref[half * 8 + q, rows_at(j, 16), :] = turned_over[q * 16 : q * 16 + 16, :]
        return 0

    lax.fori_loop(0, 32, step, 0, unroll=4)


VM = pl.BlockSpec(memory_space=pltpu.VMEM)
HB = pl.BlockSpec(memory_space=pl.ANY)


def shape(dims, kind=bf16):
    return jax.ShapeDtypeStruct(dims, kind)


def plane_steps():
    return [(s, t) for s in range(4) for t in range(4) if s or t]


FAR_FIRST = (
    (2, 2), (0, 2), (2, 0), (1, 2), (3, 2), (2, 1), (2, 3), (1, 1), (3, 3), (3, 1), (1, 3), (0, 1), (0, 3), (1, 0), (3, 0),
)


GROUPS = (
    (0, 512, 2, (0, 1)), (512, 512, 2, (0, 1)),
    (1024, 256, 1, (0, 2)), (1280, 256, 0, (1, 2)), (1536, 256, 1, (0, 2)), (1792, 256, 0, (1, 2)),
)


def remote(src, dst, ssem, rsem, to):
    return pltpu.make_async_remote_copy(
        src_ref=src, dst_ref=dst, send_sem=ssem, recv_sem=rsem, device_id=to, device_id_type=MESH
    )


class Group:
    def owners(self, body):
        if self.g == 0:
            pl.when(self.here[3] == 0)(body)
        else:
            body()

    def others(self, body):
        if self.g == 0:
            pl.when(self.here[3] == 1)(body)

    def __init__(self, g, scale, w_ref, out_ref, h_in, h_sum, q_in, q_sum, f_in, f_sum, sems):
        self.g, self.scale = g, scale
        self.w, self.out, self.h_in, self.h_sum = w_ref, out_ref, h_in, h_sum
        self.q_in, self.q_sum, self.f_in, self.f_sum = q_in, q_sum, f_in, f_sum
        self.sems = sems
        self.col, self.width, self.axis, self.plane = GROUPS[g]
        self.cols = pl.ds(self.col, self.width)
        self.out_col = self.col if g < 2 else self.col - 1024
        self.out_cols = pl.ds(self.out_col, self.width)
        self.here = coords()
        z, x, y, core = self.here
        self.mate = at(z, x, y, 1 - core)
        self.keep = pl.multiple_of(core * 512, 512)
        self.give = pl.multiple_of(512 - core * 512, 512)
        self.sent = []

    def begin(self):
        s0, r0 = self.sems[0:2]
        rows = pl.ds(self.give, 512)
        self.copy0 = remote(self.w.at[rows, self.cols], self.h_in.at[:, self.cols], s0.at[self.g], r0.at[self.g], self.mate)
        if self.g == 0:
            self.others(self.copy0.start)
        else:
            self.copy0.start()

    def to_axis(self):
        s1, r1 = self.sems[2:4]

        def add(i, _):
            rows = rows_at(i, 32)
            mine = pl.ds(pl.multiple_of(self.keep + i * 32, 32), 32)
            total = self.w[mine, self.cols].astype(f32) + self.h_in[rows, self.cols].astype(f32)
            self.h_sum[rows, self.cols] = total.astype(bf16)
            return 0

        self.copies1 = []
        for s in (2, 1, 3):
            to = turned(self.here, self.axis, s)
            rows = pl.ds(pl.multiple_of(to[self.axis] * 128, 128), 128)
            c = remote(self.h_sum.at[rows, self.cols], self.q_in.at[s - 1], s1.at[self.g, s - 1], r1.at[self.g, s - 1], at(*to))
            self.copies1.append(c)
        self.sent += self.copies1

        def body():
            if self.g:
                self.copy0.wait()
            else:
                self.copy0.wait_recv()
            lax.fori_loop(0, 16, add, 0)
            for c in self.copies1:
                c.start()

        self.others(self.copy0.wait_send)
        self.owners(body)

    def piece(self, pos):
        b = pos[self.plane[0]] * 4 + pos[self.plane[1]]
        half = self.width // 2
        return (b // 2) * 16, (b % 2) * half, half

    def to_plane(self):
        s2, r2 = self.sems[4:6]
        base = pl.multiple_of(self.here[self.axis] * 128, 128)

        def add(i, _):
            rows = rows_at(i, 16)
            total = self.h_sum[pl.ds(pl.multiple_of(base + i * 16, 16), 16), self.cols].astype(f32)
            for s in range(3):
                total = total + self.q_in[s, rows, :].astype(f32)
            self.q_sum[rows, :] = total.astype(bf16)
            return 0

        self.copies2 = []
        for n, (s, t) in enumerate(plane_steps()):
            to = turned(turned(self.here, self.plane[0], s), self.plane[1], t)
            row, col, half = self.piece(to)
            src = self.q_sum.at[pl.ds(pl.multiple_of(row, 16), 16), pl.ds(pl.multiple_of(col, 128), half)]
            c = remote(src, self.f_in.at[n], s2.at[self.g, n], r2.at[self.g, n], at(*to))
            self.copies2.append(c)
        self.sent += self.copies2

        def body():
            for c in self.copies1:
                c.wait_recv()
            lax.fori_loop(0, 8, add, 0)
            for c in self.copies2:
                c.start()

        self.owners(body)

    def from_plane(self):
        t2, u2 = self.sems[6:8]
        row, col, half = self.piece(self.here)
        own_piece = (pl.ds(pl.multiple_of(row, 16), 16), pl.ds(pl.multiple_of(col, 128), half))
        spot = self.out.at[
            pl.ds(pl.multiple_of(self.keep + self.here[self.axis] * 128 + row, 16), 16),
            pl.ds(pl.multiple_of(self.out_col + col, 128), half),
        ]
        self.copies3 = []
        for n, (s, t) in enumerate(plane_steps()):
            to = turned(turned(self.here, self.plane[0], s), self.plane[1], t)
            c = remote(self.f_sum, spot, t2.at[self.g, n], u2.at[self.g, n], at(*to))
            self.copies3.append(c)
        self.own = pltpu.make_async_copy(self.f_sum, spot, t2.at[self.g, 15])
        self.sent += self.copies3

        def body():
            for c in self.copies2:
                c.wait_recv()
            total = self.q_sum[own_piece].astype(f32)
            for n in range(15):
                total = total + self.f_in[n].astype(f32)
            self.f_sum[...] = (total * self.scale).astype(bf16)
            for c in self.copies3:
                c.start()
            self.own.start()

        self.owners(body)

    def from_axis(self):
        t1, u1 = self.sems[8:10]
        spot = self.out.at[pl.ds(pl.multiple_of(self.keep + self.here[self.axis] * 128, 128), 128), self.out_cols]
        self.copies4 = []
        for s in (2, 1, 3):
            c = remote(spot, spot, t1.at[self.g, s - 1], u1.at[self.g, s - 1], at(*turned(self.here, self.axis, s)))
            self.copies4.append(c)
        self.sent += self.copies4

        def body():
            self.own.wait()
            for c in self.copies3:
                c.wait_recv()
            for c in self.copies4:
                c.start()

        self.owners(body)

    def to_mate(self):
        t0, u0 = self.sems[10:12]
        spot = self.out.at[pl.ds(self.keep, 512), self.out_cols]
        self.copy5 = remote(spot, spot, t0.at[self.g], u0.at[self.g], self.mate)

        def body():
            for c in self.copies4:
                c.wait_recv()
            self.copy5.start()

        self.owners(body)

    def finish(self):
        def body():
            if self.g:
                self.copy5.wait()
            else:
                self.copy5.wait_send()
            for c in self.sent:
                c.wait_send()

        self.others(self.copy5.wait_recv)
        self.owners(body)


def spread_copies(pack_ref, got_ref, send, recv):
    here = coords()
    me = here[0] * 4 + here[1]
    copies = []
    for n, (s, t) in enumerate(FAR_FIRST):
        to = turned(turned(here, 0, s), 1, t)
        copies.append((to[0], remote(pack_ref.at[to[0] * 4 + to[1]], got_ref.at[me], send.at[n], recv.at[n], at(*to))))
    return copies, (here[0], pltpu.make_async_copy(pack_ref.at[me], got_ref.at[me], send.at[15]))


def started(copy, chosen):
    @pl.when(chosen)
    def _():
        copy.start()


def mover():
    l = lax.broadcasted_iota(jnp.int32, (256, 256), 0)
    n = lax.broadcasted_iota(jnp.int32, (256, 256), 1)
    swapped = jnp.where((n >= 64) & (n < 128), n + 64, jnp.where((n >= 128) & (n < 192), n - 64, n))
    return (l == swapped).astype(bf16)


def main_kernel(
    scale, psi_hbm, start_hbm, len_hbm, fine_hbm, occ_hbm, taps_hbm, magic_hbm, ext_hbm, density_ref, trial, s_ref,
    psi, start_ref, len_ref, fine_ref, occ_ref, taps, magic, ext_ref, sem_in, sem_psi,
    masked, values, part, pack_x, got, low, high, parts, wide, fine_on, weighted, bands, forward, across, pack_a, got_a,
    xt, a_t, out, x_rows, w, h_in, h_sum, *rest,
):
    q_in, q_sum, f_in, f_sum = rest[0:6], rest[6:12], rest[12:18], rest[18:24]
    sems = rest[24:36]
    sd, rd, sh, rh, sx, rx, sa, ra = rest[36:]
    here = coords()
    z, x, y, core = here
    orb, comp = lax.axis_index("orb"), lax.axis_index("comp")
    first_orbital, first_plane = orb * 64, comp * 16

    small = [
        pltpu.make_async_copy(src, dst, sem_in.at[n])
        for n, (src, dst) in enumerate(
            (
                (taps_hbm, taps), (magic_hbm, magic), (start_hbm, start_ref), (len_hbm, len_ref), (fine_hbm, fine_ref),
                (occ_hbm, occ_ref), (ext_hbm, ext_ref),
            )
        )
    ]
    for c in small:
        c.start()
    psi_copies = [
        pltpu.make_async_copy(psi_hbm.at[pl.ds(16 * n, 16)], psi.at[pl.ds(16 * n, 16)], sem_psi.at[n]) for n in range(4)
    ]
    for c in psi_copies:
        c.start()

    targets = [at(z, x, y, 1 - core), at(z, x, lax.rem(y + 3 + 2 * core, 4), 1 - core)]
    for a in (0, 1, 2):
        targets += [at(*turned(here, a, s)) for s in (1, 2, 3)]
    for a, b in ((0, 1), (0, 2), (1, 2)):
        targets += [at(*turned(turned(here, a, s), b, t)) for s in (1, 2, 3) for t in (1, 2, 3)]
    barrier = pltpu.get_barrier_semaphore()
    for t in targets:
        pl.semaphore_signal(barrier, inc=1, device_id=t, device_id_type=MESH)

    for c in small:
        c.wait()
    rows = []
    for e in range(4):
        rows.append(placed(taps[e], lambda t: lax.rem(270 - t, 256)))
    magic_rows = placed(magic[...], lambda t: lax.rem(263 - t, 256))
    adjoint_rows = placed(magic[...], lambda t: lax.rem(t + 249, 256))
    for d in range(4):
        for e in range(4):
            bands[d * 4 + e] = band(rows[e][d : d + 1])
        bands[16 + d] = band(adjoint_rows[d : d + 1])
        forward[d] = band(magic_rows[d : d + 1])
    spot = lax.rem(lax.broadcasted_iota(jnp.int32, (16, 256), 1), 48)
    edge = ((comp == 0) & (spot < 16)) | ((comp == 7) & (spot >= 32))
    for e in range(4):
        line = sum(placed(taps[e, d : d + 1], lambda t, d=d: t + (d * 48 + 2)) for d in range(4))
        rolled = pltpu.roll(jnp.broadcast_to(line, (16, 256)), 0, 1, stride=1, stride_axis=0)
        across[pl.ds(e * 16, 16), :] = jnp.where(edge, 0.0, rolled).astype(bf16)

    fine_on[...] = fine_points(fine_ref[...])
    fine = fine_on[...] > 0.5
    for n in range(4):
        psi_copies[n].wait()

        def mask(o, _):
            inside = inside_planes(start_ref, len_ref, first_orbital, first_plane, o, 256)
            for c in range(4):
                on = inside if c == 0 else inside & fine
                value = jnp.where(on, psi[o, c].astype(f32), 0.0)
                masked[o, c] = value.astype(bf16)
                spots = pl.ds(pl.multiple_of(o * 64 + c * 16, 16), 16)
                wide[spots, :] = value[:, :128]
                wide[pl.ds(pl.multiple_of(4096 + o * 64 + c * 16, 16), 16), :] = value[:, 128:]
            return 0

        lax.fori_loop(16 * n, 16 * n + 16, mask, 0, unroll=2)
    def block(i, total):
        seen = jnp.zeros((256, 256), f32)
        for d in range(4):
            seen = seen + jnp.dot(masked[rows_at(i, 16), d].reshape(256, 256), forward[d], preferred_element_type=f32)
        for n in range(16):
            one = seen[n * 16 : n * 16 + 16]
            values[i * 16 + n] = one
            total = total + occ_ref[first_orbital + i * 16 + n].astype(f32) * (one * one)
        return total

    part[...] = lax.fori_loop(0, 4, block, jnp.zeros((16, 256), f32))
    halves = (lax.rem(x, 2), 1 - lax.rem(x, 2))
    spread_x, own_x = spread_copies(pack_x, got, sx, rx)
    spread_a, own_a = spread_copies(pack_a, got_a, sa, ra)
    pack(wide, pack_x, halves[0])
    pl.semaphore_wait(barrier, len(targets))

    halo_copies = []
    halo_parts = ((0, 0, 64), (1, 0, 32), (1, 32, 32))
    for n, (m, o, count) in enumerate(halo_parts):
        spot = (pl.ds(o, count), slice(None), slice(None), pl.ds(pl.multiple_of(128 * halves[m], 128), 128))
        for k, (ref, turn) in enumerate(((low, 1), (high, 7))):
            halo_copies.append(
                remote(
                    masked.at[spot], ref.at[spot], sh.at[2 * n + k], rh.at[2 * n + k],
                    {"orb": orb, "comp": lax.rem(comp + turn, 8)},
                )
            )
    for c in halo_copies:
        c.start()

    density_copies = []
    for n, (s, t) in enumerate(FAR_FIRST):
        to = turned(turned(here, 0, s), 1, t)
        density_copies.append(remote(part, parts.at[n], sd.at[n], rd.at[n], at(*to)))
    for c in density_copies:
        c.start()

    for to_z, c in spread_x + [own_x]:
        started(c, lax.div(to_z, 2) == halves[0])
    pack(wide, pack_x, halves[1])
    for to_z, c in spread_x + [own_x]:
        started(c, lax.div(to_z, 2) == halves[1])

    density = part[...]
    for n in range(15):
        density_copies[n].wait_recv()
        density = density + parts[n]
    density_ref[...] = pltpu.roll(density, 256 - orb * 16, 1)[:, :16]
    potential = ext_ref[...] - xc_factor * jnp.exp(jnp.log(density) * (1.0 / 3.0))

    def weigh(o, _):
        weighted[o] = (potential * values[o]).astype(bf16)
        return 0

    lax.fori_loop(0, 64, weigh, 0, unroll=4)

    def along(i, _):
        for e in range(4):
            total = jnp.dot(weighted[rows_at(i, 16)].reshape(256, 256), bands[16 + e], preferred_element_type=f32)
            for d in range(4):
                total = total + jnp.dot(
                    masked[rows_at(i, 16), d].reshape(256, 256), bands[d * 4 + e], preferred_element_type=f32
                )
            for n in range(16):
                spots = pl.ds(pl.multiple_of((i * 16 + n) * 64 + e * 16, 16), 16)
                wide[spots, :] = total[n * 16 : n * 16 + 16, :128]
                spots = pl.ds(pl.multiple_of(4096 + (i * 16 + n) * 64 + e * 16, 16), 16)
                wide[spots, :] = total[n * 16 : n * 16 + 16, 128:]
        return 0

    lax.fori_loop(0, 4, along, 0)

    for n, h in enumerate(halves):
        lanes = pl.ds(pl.multiple_of(128 * h, 128), 128)
        fine_half = fine_on[:, lanes] > 0.5

        def cross(i, _, h=h, lanes=lanes, fine_half=fine_half):
            o = 2 * i
            window = jnp.concatenate(
                [
                    jnp.concatenate([ref[o, d, :, lanes], ref[o + 1, d, :, lanes]], axis=1)
                    for d in range(4)
                    for ref in (low, masked, high)
                ],
                axis=0,
            )
            summed = jnp.dot(across[:, :192], window, preferred_element_type=f32)
            for k in range(2):
                inside = inside_planes(start_ref, len_ref, first_orbital, first_plane, o + k, 128)
                for e in range(4):
                    on = inside if e == 0 else inside & fine_half
                    spots = pl.ds(pl.multiple_of(h * 4096 + (o + k) * 64 + e * 16, 16), 16)
                    term = summed[e * 16 : e * 16 + 16, 128 * k : 128 * k + 128]
                    wide[spots, :] = jnp.where(on, term + wide[spots, :], 0.0)
            return 0

        for p, (m, o, count) in enumerate(halo_parts):
            if m == n:
                for c in halo_copies[2 * p : 2 * p + 2]:
                    c.wait_recv()
                lax.fori_loop(o // 2, (o + count) // 2, cross, 0, unroll=4)
        pack(wide, pack_a, h)
        for to_z, c in spread_a + [own_a]:
            started(c, lax.div(to_z, 2) == h)

    move = mover()
    own_x[1].wait()
    for _, c in spread_x:
        c.wait_recv()

    def unpack_x(m, _):
        pair = jnp.concatenate([got[2 * m], got[2 * m + 1]], axis=1)
        turned_back = jnp.dot(pair, move, preferred_element_type=f32).astype(bf16)
        spots = pl.ds(pl.multiple_of(128 * m, 128), 128)
        xt[0:512, spots] = turned_back[:, :128]
        xt[512:1024, spots] = turned_back[:, 128:]
        across_rows = lax.dot_general(move, pair, (((1,), (1,)), ((), ())), preferred_element_type=f32).astype(bf16)
        x_rows[spots, 0:512] = across_rows[:128]
        x_rows[spots, 512:1024] = across_rows[128:]
        return 0

    lax.fori_loop(0, 8, unpack_x, 0)
    groups = [Group(g, scale, w, out if g > 1 else s_ref, h_in, h_sum, q_in[g], q_sum[g], f_in[g], f_sum[g], sems) for g in range(6)]
    corner, overlap = groups[:2]

    keep, give = pl.multiple_of(core * 512, 512), pl.multiple_of(512 - core * 512, 512)

    def products(other, col, first_row):
        def step(i, _):
            spots = pl.ds(pl.multiple_of(first_row + i * 256, 256), 256)
            w[spots, col : col + 1024] = jnp.dot(x_rows[spots, :], other[...], preferred_element_type=f32).astype(bf16)
            return 0

        lax.fori_loop(0, 2, step, 0)

    products(xt, 0, give)
    corner.begin()
    overlap.begin()
    products(xt, 0, keep)
    corner.to_axis()
    overlap.to_axis()
    corner.to_plane()
    overlap.to_plane()
    for s in (2, 1, 3, 0):
        for n, step in enumerate(FAR_FIRST):
            if step[0] == s:
                spread_a[n][1].wait_recv()
        if s == 0:
            own_a[1].wait()
        source_z = lax.rem(z + 4 - s, 4)
        for k in range(2):
            m = 2 * source_z + k
            pair = jnp.concatenate([got_a[2 * m], got_a[2 * m + 1]], axis=1)
            turned_back = jnp.dot(pair, move, preferred_element_type=f32).astype(bf16)
            spots = pl.ds(pl.multiple_of(128 * m, 128), 128)
            a_t[0:512, spots] = turned_back[:, :128]
            a_t[512:1024, spots] = turned_back[:, 128:]
    products(a_t, 1024, give)
    for group in groups[2:]:
        group.begin()
    products(a_t, 1024, keep)
    for group in groups[2:]:
        group.to_axis()
    for group in groups[2:4]:
        group.to_plane()
    corner.from_plane()
    overlap.from_plane()
    for group in groups[4:]:
        group.to_plane()
    for group in groups[2:]:
        group.from_plane()
    for group in groups[2:4]:
        group.from_axis()
    corner.from_axis()
    overlap.from_axis()
    for group in groups[4:]:
        group.from_axis()
    for group in groups[2:]:
        group.to_mate()
    for group in groups[2:]:
        group.finish()
    corner.to_mate()
    overlap.to_mate()
    for n in range(4):
        spots = pl.ds(256 * n, 256)
        mine = xt[spots, :]
        gradient = a_t[spots, :].astype(f32) - jnp.dot(mine, out[...], preferred_element_type=f32)
        trial[spots, :] = (mine.astype(f32) - step_length * gradient).astype(bf16)
    for c in density_copies + halo_copies + [c for _, c in spread_x + spread_a]:
        c.wait_send()
    corner.finish()
    overlap.finish()


def last_kernel(trial, s_all, part, next_hbm, density, following, sems):
    density[...] = part[...]
    done = []
    for n in range(4):
        rows = pl.ds(256 * n, 256)
        one, two = trial[rows, 0:512], trial[rows, 512:1024]
        left = jnp.dot(one, s_all[0:512, 0:512], preferred_element_type=f32) + lax.dot_general(
            two, s_all[0:512, 512:1024], (((1,), (1,)), ((), ())), preferred_element_type=f32
        )
        right = jnp.dot(one, s_all[0:512, 512:1024], preferred_element_type=f32) + jnp.dot(
            two, s_all[512:1024, 512:1024], preferred_element_type=f32
        )
        following[rows, 0:512] = (1.5 * one.astype(f32) - 0.5 * left).astype(bf16)
        following[rows, 512:1024] = (1.5 * two.astype(f32) - 0.5 * right).astype(bf16)
        done.append(pltpu.make_async_copy(following.at[rows], next_hbm.at[rows], sems.at[n]))
        done[-1].start()
    for c in done:
        c.wait()


def last_step(trial, s_all, part):
    return pl.pallas_call(
        last_kernel,
        out_shape=(shape((1024, 1024)), shape((16, 16), f32)),
        in_specs=[VM] * 3,
        out_specs=(pl.BlockSpec(memory_space=pltpu.HBM), VM),
        scratch_shapes=[pltpu.VMEM((1024, 1024), bf16), pltpu.SemaphoreType.DMA((4,))],
        compiler_params=pltpu.CompilerParams(vmem_limit_bytes=24 << 20),
        name="last",
    )(trial, s_all, part)


def main_step(scale, *args):
    dma = pltpu.SemaphoreType.DMA
    vm = pltpu.VMEM
    sm = pltpu.SMEM
    widths = [g[1] for g in GROUPS]
    spread_buffer = vm((16, 512, 128), bf16)
    square = vm((1024, 1024), bf16)
    orbitals = vm((64, 4, 16, 256), bf16)
    return pl.pallas_call(
        functools.partial(main_kernel, scale),
        out_shape=(shape((16, 16), f32), shape((1024, 1024)), shape((1024, 1024))),
        in_specs=[pl.BlockSpec(memory_space=pltpu.HBM)] * 8,
        out_specs=(VM,) * 3,
        scratch_shapes=[orbitals, sm((1024,), jnp.int32), sm((1024,), jnp.int32), vm((16, 16), jnp.int32)]
        + [sm((1024,), jnp.int32), vm((4, 4, 29), bf16), vm((4, 16), bf16), vm((16, 256), f32), dma((7,)), dma((4,))]
        + [orbitals, vm((64, 16, 256), f32), vm((16, 256), f32), spread_buffer, spread_buffer, orbitals, orbitals]
        + [vm((15, 16, 256), f32), vm((8192, 128), f32), vm((16, 256), f32), vm((64, 16, 256), bf16)]
        + [vm((20, 256, 256), bf16), vm((4, 256, 256), bf16), vm((64, 256), bf16), spread_buffer, spread_buffer]
        + [square, square, square, square]
        + [vm((1024, 2048), bf16), vm((512, 2048), bf16), vm((512, 2048), bf16)]
        + [vm((3, 128, n), bf16) for n in widths]
        + [vm((128, n), bf16) for n in widths]
        + [vm((15, 16, n // 2), bf16) for n in widths]
        + [vm((16, n // 2), bf16) for n in widths]
        + [dma((6,)), dma((6,)), dma((6, 3)), dma((6, 3)), dma((6, 15)), dma((6, 15))]
        + [dma((6, 16)), dma((6, 15)), dma((6, 3)), dma((6, 3)), dma((6,)), dma((6,))]
        + [dma((15,)), dma((15,)), dma((6,)), dma((6,)), dma((16,)), dma((15,)), dma((16,)), dma((15,))],
        compiler_params=pltpu.CompilerParams(collective_id=3, has_side_effects=True, vmem_limit_bytes=VMEM_MAIN),
        name="main",
    )(*[pltpu.with_memory_space_constraint(arg, pltpu.HBM) for arg in args])


VMEM_MAIN = 47 << 20


def local(psi, region_start, region_len, fine_mask, occupation, kinetic_taps, magic_taps, external):
    density, trial, intersection = main_step(
        1.0 / 32768, psi, region_start, region_len, fine_mask, occupation,
        jnp.transpose(kinetic_taps, (1, 2, 0)), jnp.transpose(magic_taps), external,
    )
    following, density = last_step(trial, intersection, density)
    return (density, jnp.transpose(following.reshape(4, 16, 16, 1024), (3, 0, 1, 2)))


def solution(mesh):
    return jax.shard_map(
        local,
        mesh=mesh,
        in_specs=(
            P("orb", None, "comp", None),
            P(),
            P(),
            P("comp", None),
            P(),
            P(),
            P(),
            P("comp", None),
        ),
        out_specs=(P("comp", "orb"), P(None, None, "comp", "orb")),
        check_vma=False,
    )
```

```python
import functools

import jax
import jax.numpy as jnp
from jax import lax
from jax.experimental import pallas as pl
from jax.experimental.pallas import tpu as pltpu
from jax.sharding import PartitionSpec as P

ZB = 16
xc_factor = 0.98474502
step_length = 0.1
f32, bf16 = jnp.float32, jnp.bfloat16

MESH = pl.DeviceIdType.MESH


def coords():
    orb, comp = lax.axis_index("orb"), lax.axis_index("comp")
    return orb // 4, orb % 4, comp // 2, comp % 2


def at(z, x, y, core):
    return {"orb": z * 4 + x, "comp": y * 2 + core}


def turned(pos, axis, step):
    pos = list(pos)
    pos[axis] = lax.rem(pos[axis] + step, 4)
    return tuple(pos)


def rows_at(i, size):
    return pl.ds(pl.multiple_of(i * size, size), size)


def eye(n):
    return (
        lax.broadcasted_iota(jnp.int32, (n, n), 0) == lax.broadcasted_iota(jnp.int32, (n, n), 1)
    ).astype(bf16)


def band(row):
    wide = jnp.broadcast_to(row, (256, 256))
    rolled = pltpu.roll(wide, 0, 1, stride=1, stride_axis=0)
    gap = lax.broadcasted_iota(jnp.int32, (256, 256), 0) - lax.broadcasted_iota(jnp.int32, (256, 256), 1)
    return jnp.where((gap <= 14) & (gap >= -14), rolled, 0.0).astype(bf16)


def inside_planes(start_ref, len_ref, first_orbital, first_plane, o, width):
    begin = start_ref[first_orbital + o] - first_plane
    plane = lax.broadcasted_iota(jnp.int32, (16, width), 0)
    return (plane >= begin) & (plane < begin + len_ref[first_orbital + o])


def fine_points(fine):
    spread = (
        lax.broadcasted_iota(jnp.int32, (16, 256), 1) // ZB == lax.broadcasted_iota(jnp.int32, (16, 256), 0)
    ).astype(bf16)
    return jnp.dot((fine > 0).astype(f32).astype(bf16), spread, preferred_element_type=f32)


def placed(rows, spot):
    taps = rows.shape[1]
    t = lax.broadcasted_iota(jnp.int32, (taps, 256), 0)
    lane = lax.broadcasted_iota(jnp.int32, (taps, 256), 1)
    return jnp.dot(rows, (lane == spot(t)).astype(bf16), preferred_element_type=f32)


def pack(wide, pack_ref, half):
    unit = eye(128)

    def step(j, _):
        row = half * 4096 + j
        both = jnp.concatenate([wide[pl.ds(row, 64, stride=64), :], wide[pl.ds(row + 32, 64, stride=64), :]], axis=0)
        turned_over = lax.dot_general(
            unit, both.astype(bf16), (((1,), (1,)), ((), ())), preferred_element_type=f32
        ).astype(bf16)
        for q in range(8):
            pack_ref[half * 8 + q, rows_at(j, 16), :] = turned_over[q * 16 : q * 16 + 16, :]
        return 0

    lax.fori_loop(0, 32, step, 0, unroll=4)


VM = pl.BlockSpec(memory_space=pltpu.VMEM)
HB = pl.BlockSpec(memory_space=pl.ANY)


def shape(dims, kind=bf16):
    return jax.ShapeDtypeStruct(dims, kind)


def plane_steps():
    return [(s, t) for s in range(4) for t in range(4) if s or t]


FAR_FIRST = (
    (2, 2), (0, 2), (2, 0), (1, 2), (3, 2), (2, 1), (2, 3), (1, 1), (3, 3), (3, 1), (1, 3), (0, 1), (0, 3), (1, 0), (3, 0),
)


GROUPS = (
    (0, 512, 2, (0, 1)), (512, 512, 2, (0, 1)),
    (1024, 256, 1, (0, 2)), (1280, 256, 0, (1, 2)), (1536, 256, 1, (0, 2)), (1792, 256, 0, (1, 2)),
)


def remote(src, dst, ssem, rsem, to):
    return pltpu.make_async_remote_copy(
        src_ref=src, dst_ref=dst, send_sem=ssem, recv_sem=rsem, device_id=to, device_id_type=MESH
    )


class Group:
    def owners(self, body):
        if self.g == 0:
            pl.when(self.here[3] == 0)(body)
        else:
            body()

    def others(self, body):
        if self.g == 0:
            pl.when(self.here[3] == 1)(body)

    def __init__(self, g, scale, w_ref, out_ref, h_in, h_sum, q_in, q_sum, f_in, f_sum, sems):
        self.g, self.scale = g, scale
        self.w, self.out, self.h_in, self.h_sum = w_ref, out_ref, h_in, h_sum
        self.q_in, self.q_sum, self.f_in, self.f_sum = q_in, q_sum, f_in, f_sum
        self.sems = sems
        self.col, self.width, self.axis, self.plane = GROUPS[g]
        self.cols = pl.ds(self.col, self.width)
        self.out_col = self.col if g < 2 else self.col - 1024
        self.out_cols = pl.ds(self.out_col, self.width)
        self.here = coords()
        z, x, y, core = self.here
        self.mate = at(z, x, y, 1 - core)
        self.keep = pl.multiple_of(core * 512, 512)
        self.give = pl.multiple_of(512 - core * 512, 512)
        self.sent = []

    def begin(self):
        s0, r0 = self.sems[0:2]
        rows = pl.ds(self.give, 512)
        self.copy0 = remote(self.w.at[rows, self.cols], self.h_in.at[:, self.cols], s0.at[self.g], r0.at[self.g], self.mate)
        if self.g == 0:
            self.others(self.copy0.start)
        else:
            self.copy0.start()

    def to_axis(self):
        s1, r1 = self.sems[2:4]

        def add(i, _):
            rows = rows_at(i, 32)
            mine = pl.ds(pl.multiple_of(self.keep + i * 32, 32), 32)
            total = self.w[mine, self.cols].astype(f32) + self.h_in[rows, self.cols].astype(f32)
            self.h_sum[rows, self.cols] = total.astype(bf16)
            return 0

        self.copies1 = []
        for s in (2, 1, 3):
            to = turned(self.here, self.axis, s)
            rows = pl.ds(pl.multiple_of(to[self.axis] * 128, 128), 128)
            c = remote(self.h_sum.at[rows, self.cols], self.q_in.at[s - 1], s1.at[self.g, s - 1], r1.at[self.g, s - 1], at(*to))
            self.copies1.append(c)
        self.sent += self.copies1

        def body():
            if self.g:
                self.copy0.wait()
            else:
                self.copy0.wait_recv()
            lax.fori_loop(0, 16, add, 0)
            for c in self.copies1:
                c.start()

        self.others(self.copy0.wait_send)
        self.owners(body)

    def piece(self, pos):
        b = pos[self.plane[0]] * 4 + pos[self.plane[1]]
        half = self.width // 2
        return (b // 2) * 16, (b % 2) * half, half

    def to_plane(self):
        s2, r2 = self.sems[4:6]
        base = pl.multiple_of(self.here[self.axis] * 128, 128)

        def add(i, _):
            rows = rows_at(i, 16)
            total = self.h_sum[pl.ds(pl.multiple_of(base + i * 16, 16), 16), self.cols].astype(f32)
            for s in range(3):
                total = total + self.q_in[s, rows, :].astype(f32)
            self.q_sum[rows, :] = total.astype(bf16)
            return 0

        self.copies2 = []
        for n, (s, t) in enumerate(plane_steps()):
            to = turned(turned(self.here, self.plane[0], s), self.plane[1], t)
            row, col, half = self.piece(to)
            src = self.q_sum.at[pl.ds(pl.multiple_of(row, 16), 16), pl.ds(pl.multiple_of(col, 128), half)]
            c = remote(src, self.f_in.at[n], s2.at[self.g, n], r2.at[self.g, n], at(*to))
            self.copies2.append(c)
        self.sent += self.copies2

        def body():
            for c in self.copies1:
                c.wait_recv()
            lax.fori_loop(0, 8, add, 0)
            for c in self.copies2:
                c.start()

        self.owners(body)

    def from_plane(self):
        t2, u2 = self.sems[6:8]
        row, col, half = self.piece(self.here)
        own_piece = (pl.ds(pl.multiple_of(row, 16), 16), pl.ds(pl.multiple_of(col, 128), half))
        spot = self.out.at[
            pl.ds(pl.multiple_of(self.keep + self.here[self.axis] * 128 + row, 16), 16),
            pl.ds(pl.multiple_of(self.out_col + col, 128), half),
        ]
        self.copies3 = []
        for n, (s, t) in enumerate(plane_steps()):
            to = turned(turned(self.here, self.plane[0], s), self.plane[1], t)
            c = remote(self.f_sum, spot, t2.at[self.g, n], u2.at[self.g, n], at(*to))
            self.copies3.append(c)
        self.own = pltpu.make_async_copy(self.f_sum, spot, t2.at[self.g, 15])
        self.sent += self.copies3

        def body():
            for c in self.copies2:
                c.wait_recv()
            total = self.q_sum[own_piece].astype(f32)
            for n in range(15):
                total = total + self.f_in[n].astype(f32)
            self.f_sum[...] = (total * self.scale).astype(bf16)
            for c in self.copies3:
                c.start()
            self.own.start()

        self.owners(body)

    def from_axis(self):
        t1, u1 = self.sems[8:10]
        spot = self.out.at[pl.ds(pl.multiple_of(self.keep + self.here[self.axis] * 128, 128), 128), self.out_cols]
        self.copies4 = []
        for s in (2, 1, 3):
            c = remote(spot, spot, t1.at[self.g, s - 1], u1.at[self.g, s - 1], at(*turned(self.here, self.axis, s)))
            self.copies4.append(c)
        self.sent += self.copies4

        def body():
            self.own.wait()
            for c in self.copies3:
                c.wait_recv()
            for c in self.copies4:
                c.start()

        self.owners(body)

    def to_mate(self):
        t0, u0 = self.sems[10:12]
        spot = self.out.at[pl.ds(self.keep, 512), self.out_cols]
        self.copy5 = remote(spot, spot, t0.at[self.g], u0.at[self.g], self.mate)

        def body():
            for c in self.copies4:
                c.wait_recv()
            self.copy5.start()

        self.owners(body)

    def finish(self):
        def body():
            if self.g:
                self.copy5.wait()
            else:
                self.copy5.wait_send()
            for c in self.sent:
                c.wait_send()

        self.others(self.copy5.wait_recv)
        self.owners(body)


def spread_copies(pack_ref, got_ref, send, recv):
    here = coords()
    me = here[0] * 4 + here[1]
    copies = []
    for n, (s, t) in enumerate(FAR_FIRST):
        to = turned(turned(here, 0, s), 1, t)
        copies.append((to[0], remote(pack_ref.at[to[0] * 4 + to[1]], got_ref.at[me], send.at[n], recv.at[n], at(*to))))
    return copies, (here[0], pltpu.make_async_copy(pack_ref.at[me], got_ref.at[me], send.at[15]))


def started(copy, chosen):
    @pl.when(chosen)
    def _():
        copy.start()


def mover():
    l = lax.broadcasted_iota(jnp.int32, (256, 256), 0)
    n = lax.broadcasted_iota(jnp.int32, (256, 256), 1)
    swapped = jnp.where((n >= 64) & (n < 128), n + 64, jnp.where((n >= 128) & (n < 192), n - 64, n))
    return (l == swapped).astype(bf16)


def main_kernel(
    scale, psi_hbm, start_hbm, len_hbm, fine_hbm, occ_hbm, taps_hbm, magic_hbm, ext_hbm, density_ref, trial, s_ref,
    psi, start_ref, len_ref, fine_ref, occ_ref, taps, magic, ext_ref, sem_in, sem_psi,
    masked, values, part, pack_x, got, low, high, parts, wide, fine_on, weighted, bands, forward, across, pack_a, got_a,
    xt, a_t, out, x_rows, w, h_in, h_sum, *rest,
):
    q_in, q_sum, f_in, f_sum = rest[0:6], rest[6:12], rest[12:18], rest[18:24]
    sems = rest[24:36]
    sd, rd, sh, rh, sx, rx, sa, ra = rest[36:]
    here = coords()
    z, x, y, core = here
    orb, comp = lax.axis_index("orb"), lax.axis_index("comp")
    first_orbital, first_plane = orb * 64, comp * 16

    small = [
        pltpu.make_async_copy(src, dst, sem_in.at[n])
        for n, (src, dst) in enumerate(
            (
                (taps_hbm, taps), (magic_hbm, magic), (start_hbm, start_ref), (len_hbm, len_ref), (fine_hbm, fine_ref),
                (occ_hbm, occ_ref), (ext_hbm, ext_ref),
            )
        )
    ]
    for c in small:
        c.start()
    psi_copies = [
        pltpu.make_async_copy(psi_hbm.at[pl.ds(16 * n, 16)], psi.at[pl.ds(16 * n, 16)], sem_psi.at[n]) for n in range(4)
    ]
    for c in psi_copies:
        c.start()

    targets = [at(z, x, y, 1 - core), at(z, x, lax.rem(y + 3 + 2 * core, 4), 1 - core)]
    for a in (0, 1, 2):
        targets += [at(*turned(here, a, s)) for s in (1, 2, 3)]
    for a, b in ((0, 1), (0, 2), (1, 2)):
        targets += [at(*turned(turned(here, a, s), b, t)) for s in (1, 2, 3) for t in (1, 2, 3)]
    barrier = pltpu.get_barrier_semaphore()
    for t in targets:
        pl.semaphore_signal(barrier, inc=1, device_id=t, device_id_type=MESH)

    for c in small:
        c.wait()
    rows = []
    for e in range(4):
        rows.append(placed(taps[e], lambda t: lax.rem(270 - t, 256)))
    magic_rows = placed(magic[...], lambda t: lax.rem(263 - t, 256))
    adjoint_rows = placed(magic[...], lambda t: lax.rem(t + 249, 256))
    for d in range(4):
        for e in range(4):
            bands[d * 4 + e] = band(rows[e][d : d + 1])
        bands[16 + d] = band(adjoint_rows[d : d + 1])
        forward[d] = band(magic_rows[d : d + 1])
    spot = lax.rem(lax.broadcasted_iota(jnp.int32, (16, 256), 1), 48)
    edge = ((comp == 0) & (spot < 16)) | ((comp == 7) & (spot >= 32))
    for e in range(4):
        line = sum(placed(taps[e, d : d + 1], lambda t, d=d: t + (d * 48 + 2)) for d in range(4))
        rolled = pltpu.roll(jnp.broadcast_to(line, (16, 256)), 0, 1, stride=1, stride_axis=0)
        across[pl.ds(e * 16, 16), :] = jnp.where(edge, 0.0, rolled).astype(bf16)

    fine_on[...] = fine_points(fine_ref[...])
    fine = fine_on[...] > 0.5
    for n in range(4):
        psi_copies[n].wait()

        def mask(o, _):
            inside = inside_planes(start_ref, len_ref, first_orbital, first_plane, o, 256)
            for c in range(4):
                on = inside if c == 0 else inside & fine
                value = jnp.where(on, psi[o, c].astype(f32), 0.0)
                masked[o, c] = value.astype(bf16)
                spots = pl.ds(pl.multiple_of(o * 64 + c * 16, 16), 16)
                wide[spots, :] = value[:, :128]
                wide[pl.ds(pl.multiple_of(4096 + o * 64 + c * 16, 16), 16), :] = value[:, 128:]
            return 0

        lax.fori_loop(16 * n, 16 * n + 16, mask, 0, unroll=2)
    def block(i, total):
        seen = jnp.zeros((256, 256), f32)
        for d in range(4):
            seen = seen + jnp.dot(masked[rows_at(i, 16), d].reshape(256, 256), forward[d], preferred_element_type=f32)
        for n in range(16):
            one = seen[n * 16 : n * 16 + 16]
            values[i * 16 + n] = one
            total = total + occ_ref[first_orbital + i * 16 + n].astype(f32) * (one * one)
        return total

    part[...] = lax.fori_loop(0, 4, block, jnp.zeros((16, 256), f32))
    halves = (lax.rem(x, 2), 1 - lax.rem(x, 2))
    spread_x, own_x = spread_copies(pack_x, got, sx, rx)
    spread_a, own_a = spread_copies(pack_a, got_a, sa, ra)
    pack(wide, pack_x, halves[0])
    pl.semaphore_wait(barrier, len(targets))

    halo_copies = []
    halo_parts = ((0, 0, 64), (1, 0, 32), (1, 32, 32))
    for n, (m, o, count) in enumerate(halo_parts):
        spot = (pl.ds(o, count), slice(None), slice(None), pl.ds(pl.multiple_of(128 * halves[m], 128), 128))
        for k, (ref, turn) in enumerate(((low, 1), (high, 7))):
            halo_copies.append(
                remote(
                    masked.at[spot], ref.at[spot], sh.at[2 * n + k], rh.at[2 * n + k],
                    {"orb": orb, "comp": lax.rem(comp + turn, 8)},
                )
            )
    for c in halo_copies:
        c.start()

    density_copies = []
    for n, (s, t) in enumerate(FAR_FIRST):
        to = turned(turned(here, 0, s), 1, t)
        density_copies.append(remote(part, parts.at[n], sd.at[n], rd.at[n], at(*to)))
    for c in density_copies:
        c.start()

    for to_z, c in spread_x + [own_x]:
        started(c, lax.div(to_z, 2) == halves[0])
    pack(wide, pack_x, halves[1])
    for to_z, c in spread_x + [own_x]:
        started(c, lax.div(to_z, 2) == halves[1])

    def along(i, _):
        for e in range(4):
            total = jnp.zeros((256, 256), f32)
            for d in range(4):
                total = total + jnp.dot(
                    masked[rows_at(i, 16), d].reshape(256, 256), bands[d * 4 + e], preferred_element_type=f32
                )
            for n in range(16):
                spots = pl.ds(pl.multiple_of((i * 16 + n) * 64 + e * 16, 16), 16)
                wide[spots, :] = total[n * 16 : n * 16 + 16, :128]
                spots = pl.ds(pl.multiple_of(4096 + (i * 16 + n) * 64 + e * 16, 16), 16)
                wide[spots, :] = total[n * 16 : n * 16 + 16, 128:]
        return 0

    lax.fori_loop(0, 4, along, 0)
    density = part[...]
    for n in range(15):
        density_copies[n].wait_recv()
        density = density + parts[n]
    density_ref[...] = pltpu.roll(density, 256 - orb * 16, 1)[:, :16]
    potential = ext_ref[...] - xc_factor * jnp.exp(jnp.log(density) * (1.0 / 3.0))

    def weigh(o, _):
        weighted[o] = (potential * values[o]).astype(bf16)
        return 0

    lax.fori_loop(0, 64, weigh, 0, unroll=4)

    def adjoint(i, _):
        for e in range(4):
            total = jnp.dot(weighted[rows_at(i, 16)].reshape(256, 256), bands[16 + e], preferred_element_type=f32)
            for n in range(16):
                spots = pl.ds(pl.multiple_of((i * 16 + n) * 64 + e * 16, 16), 16)
                wide[spots, :] += total[n * 16 : n * 16 + 16, :128]
                spots = pl.ds(pl.multiple_of(4096 + (i * 16 + n) * 64 + e * 16, 16), 16)
                wide[spots, :] += total[n * 16 : n * 16 + 16, 128:]
        return 0

    lax.fori_loop(0, 4, adjoint, 0)

    for n, h in enumerate(halves):
        lanes = pl.ds(pl.multiple_of(128 * h, 128), 128)
        fine_half = fine_on[:, lanes] > 0.5

        def cross(i, _, h=h, lanes=lanes, fine_half=fine_half):
            o = 2 * i
            window = jnp.concatenate(
                [
                    jnp.concatenate([ref[o, d, :, lanes], ref[o + 1, d, :, lanes]], axis=1)
                    for d in range(4)
                    for ref in (low, masked, high)
                ],
                axis=0,
            )
            summed = jnp.dot(across[:, :192], window, preferred_element_type=f32)
            for k in range(2):
                inside = inside_planes(start_ref, len_ref, first_orbital, first_plane, o + k, 128)
                for e in range(4):
                    on = inside if e == 0 else inside & fine_half
                    spots = pl.ds(pl.multiple_of(h * 4096 + (o + k) * 64 + e * 16, 16), 16)
                    term = summed[e * 16 : e * 16 + 16, 128 * k : 128 * k + 128]
                    wide[spots, :] = jnp.where(on, term + wide[spots, :], 0.0)
            return 0

        for p, (m, o, count) in enumerate(halo_parts):
            if m == n:
                for c in halo_copies[2 * p : 2 * p + 2]:
                    c.wait_recv()
                lax.fori_loop(o // 2, (o + count) // 2, cross, 0, unroll=4)
        pack(wide, pack_a, h)
        for to_z, c in spread_a + [own_a]:
            started(c, lax.div(to_z, 2) == h)

    move = mover()
    own_x[1].wait()
    for _, c in spread_x:
        c.wait_recv()

    def unpack_x(m, _):
        pair = jnp.concatenate([got[2 * m], got[2 * m + 1]], axis=1)
        turned_back = jnp.dot(pair, move, preferred_element_type=f32).astype(bf16)
        spots = pl.ds(pl.multiple_of(128 * m, 128), 128)
        xt[0:512, spots] = turned_back[:, :128]
        xt[512:1024, spots] = turned_back[:, 128:]
        across_rows = lax.dot_general(move, pair, (((1,), (1,)), ((), ())), preferred_element_type=f32).astype(bf16)
        x_rows[spots, 0:512] = across_rows[:128]
        x_rows[spots, 512:1024] = across_rows[128:]
        return 0

    lax.fori_loop(0, 8, unpack_x, 0)
    groups = [Group(g, scale, w, out if g > 1 else s_ref, h_in, h_sum, q_in[g], q_sum[g], f_in[g], f_sum[g], sems) for g in range(6)]
    corner, overlap = groups[:2]

    keep, give = pl.multiple_of(core * 512, 512), pl.multiple_of(512 - core * 512, 512)

    def products(other, col, first_row):
        def step(i, _):
            spots = pl.ds(pl.multiple_of(first_row + i * 256, 256), 256)
            w[spots, col : col + 1024] = jnp.dot(x_rows[spots, :], other[...], preferred_element_type=f32).astype(bf16)
            return 0

        lax.fori_loop(0, 2, step, 0)

    products(xt, 0, give)
    corner.begin()
    overlap.begin()
    products(xt, 0, keep)
    corner.to_axis()
    overlap.to_axis()
    corner.to_plane()
    overlap.to_plane()
    for s in (2, 1, 3, 0):
        for n, step in enumerate(FAR_FIRST):
            if step[0] == s:
                spread_a[n][1].wait_recv()
        if s == 0:
            own_a[1].wait()
        source_z = lax.rem(z + 4 - s, 4)
        for k in range(2):
            m = 2 * source_z + k
            pair = jnp.concatenate([got_a[2 * m], got_a[2 * m + 1]], axis=1)
            turned_back = jnp.dot(pair, move, preferred_element_type=f32).astype(bf16)
            spots = pl.ds(pl.multiple_of(128 * m, 128), 128)
            a_t[0:512, spots] = turned_back[:, :128]
            a_t[512:1024, spots] = turned_back[:, 128:]
    products(a_t, 1024, give)
    for group in groups[2:]:
        group.begin()
    products(a_t, 1024, keep)
    for group in groups[2:]:
        group.to_axis()
    for group in groups[2:4]:
        group.to_plane()
    corner.from_plane()
    overlap.from_plane()
    for group in groups[4:]:
        group.to_plane()
    for group in groups[2:]:
        group.from_plane()
    for group in groups[2:4]:
        group.from_axis()
    corner.from_axis()
    overlap.from_axis()
    for group in groups[4:]:
        group.from_axis()
    for group in groups[2:]:
        group.to_mate()
    for group in groups[2:]:
        group.finish()
    corner.to_mate()
    overlap.to_mate()
    for n in range(4):
        spots = pl.ds(256 * n, 256)
        mine = xt[spots, :]
        gradient = a_t[spots, :].astype(f32) - jnp.dot(mine, out[...], preferred_element_type=f32)
        trial[spots, :] = (mine.astype(f32) - step_length * gradient).astype(bf16)
    for c in density_copies + halo_copies + [c for _, c in spread_x + spread_a]:
        c.wait_send()
    corner.finish()
    overlap.finish()


def last_kernel(trial, s_all, part, next_hbm, density, following, sems):
    density[...] = part[...]
    done = []
    for n in range(4):
        rows = pl.ds(256 * n, 256)
        one, two = trial[rows, 0:512], trial[rows, 512:1024]
        left = jnp.dot(one, s_all[0:512, 0:512], preferred_element_type=f32) + lax.dot_general(
            two, s_all[0:512, 512:1024], (((1,), (1,)), ((), ())), preferred_element_type=f32
        )
        right = jnp.dot(one, s_all[0:512, 512:1024], preferred_element_type=f32) + jnp.dot(
            two, s_all[512:1024, 512:1024], preferred_element_type=f32
        )
        following[rows, 0:512] = (1.5 * one.astype(f32) - 0.5 * left).astype(bf16)
        following[rows, 512:1024] = (1.5 * two.astype(f32) - 0.5 * right).astype(bf16)
        done.append(pltpu.make_async_copy(following.at[rows], next_hbm.at[rows], sems.at[n]))
        done[-1].start()
    for c in done:
        c.wait()


def last_step(trial, s_all, part):
    return pl.pallas_call(
        last_kernel,
        out_shape=(shape((1024, 1024)), shape((16, 16), f32)),
        in_specs=[VM] * 3,
        out_specs=(pl.BlockSpec(memory_space=pltpu.HBM), VM),
        scratch_shapes=[pltpu.VMEM((1024, 1024), bf16), pltpu.SemaphoreType.DMA((4,))],
        compiler_params=pltpu.CompilerParams(vmem_limit_bytes=24 << 20),
        name="last",
    )(trial, s_all, part)


def main_step(scale, *args):
    dma = pltpu.SemaphoreType.DMA
    vm = pltpu.VMEM
    sm = pltpu.SMEM
    widths = [g[1] for g in GROUPS]
    spread_buffer = vm((16, 512, 128), bf16)
    square = vm((1024, 1024), bf16)
    orbitals = vm((64, 4, 16, 256), bf16)
    return pl.pallas_call(
        functools.partial(main_kernel, scale),
        out_shape=(shape((16, 16), f32), shape((1024, 1024)), shape((1024, 1024))),
        in_specs=[pl.BlockSpec(memory_space=pltpu.HBM)] * 8,
        out_specs=(VM,) * 3,
        scratch_shapes=[orbitals, sm((1024,), jnp.int32), sm((1024,), jnp.int32), vm((16, 16), jnp.int32)]
        + [sm((1024,), jnp.int32), vm((4, 4, 29), bf16), vm((4, 16), bf16), vm((16, 256), f32), dma((7,)), dma((4,))]
        + [orbitals, vm((64, 16, 256), f32), vm((16, 256), f32), spread_buffer, spread_buffer, orbitals, orbitals]
        + [vm((15, 16, 256), f32), vm((8192, 128), f32), vm((16, 256), f32), vm((64, 16, 256), bf16)]
        + [vm((20, 256, 256), bf16), vm((4, 256, 256), bf16), vm((64, 256), bf16), spread_buffer, spread_buffer]
        + [square, square, square, square]
        + [vm((1024, 2048), bf16), vm((512, 2048), bf16), vm((512, 2048), bf16)]
        + [vm((3, 128, n), bf16) for n in widths]
        + [vm((128, n), bf16) for n in widths]
        + [vm((15, 16, n // 2), bf16) for n in widths]
        + [vm((16, n // 2), bf16) for n in widths]
        + [dma((6,)), dma((6,)), dma((6, 3)), dma((6, 3)), dma((6, 15)), dma((6, 15))]
        + [dma((6, 16)), dma((6, 15)), dma((6, 3)), dma((6, 3)), dma((6,)), dma((6,))]
        + [dma((15,)), dma((15,)), dma((6,)), dma((6,)), dma((16,)), dma((15,)), dma((16,)), dma((15,))],
        compiler_params=pltpu.CompilerParams(collective_id=3, has_side_effects=True, vmem_limit_bytes=VMEM_MAIN),
        name="main",
    )(*[pltpu.with_memory_space_constraint(arg, pltpu.HBM) for arg in args])


VMEM_MAIN = 47 << 20


def local(psi, region_start, region_len, fine_mask, occupation, kinetic_taps, magic_taps, external):
    density, trial, intersection = main_step(
        1.0 / 32768, psi, region_start, region_len, fine_mask, occupation,
        jnp.transpose(kinetic_taps, (1, 2, 0)), jnp.transpose(magic_taps), external,
    )
    following, density = last_step(trial, intersection, density)
    return (density, jnp.transpose(following.reshape(4, 16, 16, 1024), (3, 0, 1, 2)))


def solution(mesh):
    return jax.shard_map(
        local,
        mesh=mesh,
        in_specs=(
            P("orb", None, "comp", None),
            P(),
            P(),
            P("comp", None),
            P(),
            P(),
            P(),
            P("comp", None),
        ),
        out_specs=(P("comp", "orb"), P(None, None, "comp", "orb")),
        check_vma=False,
    )
```
